32 devices in a mesh: tile: 16 (over z, y, x), day: 2 (over core).
Axes of the slice: x: 2, y: 2, z: 4, core: 2. Of those that a mesh axis runs over, the one named last changes fastest.
Arguments:
- spectra: bfloat16 [2, 4096, 2, 4, 512], P('day', 'tile'), may hold values from -500 to 500
- band_low: int32 [32], P('tile'), may hold values from 0 to 127
- band_high: int32 [32], P('tile'), may hold values from 384 to 512
- pair_list: int32 [64, 2], P('tile'), may hold values from -1 to 31, as said below
Outputs:
- correlations: float32 [2, 64, 128, 128], P('day', 'tile')
The draws below stay inside these ranges and needn't reach their ends.
Inputs may be any that keep to these rules, and one draw needn't show every extreme that they name: `pair_list`: row p is either a pair (a, b) with 2 * (p // 4) <= a < 2 * (p // 4) + 2 and 0 <= b - a <= 6, or (-1, -1). In each aligned run of 4 rows the pairs come first, there is at least one, and in every draw some run holds 4 pairs.
All inputs are finite; a program needn't handle non-finite values.
Results may differ from the reference program's by a relative error of at most 0.0027.
Values may be sent and summed in bfloat16 or wider, within the bound.
A program may use at most 128 MiB of HBM per device.

```python
import math
import jax
import jax.numpy as jnp
from jax import lax

BLOCK = 128
BLK_DEV = 2
NF = 512
SEGLEN = 15000
FIRST = 90
HALF_WIN = 64
SEGS = 4
MAXOFF = 6
PAIR_DEV = 4
LSTEP = 25
NB = 32
CHANNELS = 4096
PAIRS = 64
DAYS = 2
LAGS = 2


def draw_spectra(key, part):
    first_key, second_key, third_key = jax.random.split(key, 3)
    full_shape = (DAYS, CHANNELS, 2, SEGS, NF)
    base_values = jnp.clip(jax.random.normal(first_key, full_shape, jnp.float32), -5.0, 5.0)
    log_range = jnp.log(10.0)
    row_scale = jnp.exp(jax.random.uniform(second_key, (DAYS, CHANNELS, 1, SEGS, 1), jnp.float32) * log_range)
    bin_scale = jnp.exp(jax.random.uniform(third_key, (DAYS, 1, 1, 1, NF), jnp.float32) * log_range)
    return (base_values * row_scale * bin_scale).astype(jnp.bfloat16)


def draw_pair_list(key, part):
    first_key, second_key, third_key, fourth_key = jax.random.split(key, 4)
    tile_count = NB // BLK_DEV
    row_index = jnp.arange(PAIRS, dtype=jnp.int32)
    tile_of_row = row_index // PAIR_DEV
    slot_of_row = row_index % PAIR_DEV
    live_counts = jax.random.randint(first_key, (tile_count,), 1, PAIR_DEV + 1)
    full_tile = jax.random.randint(second_key, (), 0, tile_count)
    live_counts = jnp.where(jnp.arange(tile_count, dtype=jnp.int32) == full_tile, PAIR_DEV, live_counts)
    first_block = BLK_DEV * tile_of_row + jax.random.randint(third_key, (PAIRS,), 0, BLK_DEV)
    second_block = jnp.minimum(first_block + jax.random.randint(fourth_key, (PAIRS,), 0, MAXOFF + 1), NB - 1)
    valid = slot_of_row < live_counts[tile_of_row]
    return jnp.stack([jnp.where(valid, first_block, -1), jnp.where(valid, second_block, -1)], axis=1).astype(jnp.int32)


def touch_ends(values, own_key, smallest, largest):
    spot = [jax.random.randint(jax.random.fold_in(own_key, axis), (), 0, length) for axis, length in enumerate(values.shape)]
    longest = values.shape.index(max(values.shape))
    beside = spot[:longest] + [(spot[longest] + 1) % values.shape[longest]] + spot[longest + 1:]
    return values.at[tuple(spot)].set(smallest).at[tuple(beside)].set(largest)


def setup_inputs(seed: int = 0) -> dict:
    arg_keys = jax.random.split(jax.random.key(seed), 5)
    return {
        "spectra": draw_spectra(jax.random.fold_in(arg_keys[4], 71), 0),
        "band_low": touch_ends(jax.random.randint(arg_keys[1], (NB,), 0, NF // 4), jax.random.fold_in(arg_keys[1], 1), 0, (NF // 4) - 1).astype(jnp.int32),
        "band_high": touch_ends(jax.random.randint(arg_keys[2], (NB,), 3 * NF // 4, NF + 1), jax.random.fold_in(arg_keys[2], 1), 3 * NF // 4, NF).astype(jnp.int32),
        "pair_list": draw_pair_list(jax.random.fold_in(arg_keys[4], 71), 0),
    }


def spread_mean(magnitude, bin_count):
    bin_index = jnp.arange(bin_count, dtype=jnp.int32)
    spread_matrix = (jnp.abs(bin_index[:, None] - bin_index[None, :]) <= HALF_WIN).astype(jnp.float32)
    bin_counts = lax.optimization_barrier(jnp.sum(spread_matrix, axis=0))
    flattened = magnitude.reshape(-1, bin_count)
    window_sums = jnp.dot(flattened, spread_matrix, precision=lax.Precision.HIGHEST)
    return (window_sums / bin_counts).reshape(magnitude.shape) + 1e-05

def whiten(raw):
    values = raw.astype(jnp.float32)
    magnitude = jnp.sqrt(values[:, 0] * values[:, 0] + values[:, 1] * values[:, 1])
    amplitude = spread_mean(magnitude, raw.shape[-1])
    return (values / amplitude[:, None]).astype(jnp.bfloat16)

def phase_tables(first_lag, lag_total, all_lags, bin_count):
    lag_index = first_lag + jnp.arange(lag_total, dtype=jnp.int32)
    lag_samples = (lag_index - all_lags // 2) * LSTEP
    bin_number = FIRST + jnp.arange(bin_count, dtype=jnp.int32)
    phase_turns = lag_samples[:, None] * bin_number[None, :] % SEGLEN
    phase_angle = phase_turns.astype(jnp.float32) * (2.0 * math.pi / SEGLEN)
    return (jnp.cos(phase_angle), jnp.sin(phase_angle))

def reference(spectra, band_low, band_high, pair_list):
    whitened = lax.map(whiten, spectra)
    blocks = whitened.reshape(DAYS, NB, BLOCK, 2, SEGS, NF)
    bin_index = jnp.arange(NF, dtype=jnp.int32)
    keep_mask = ((bin_index[None, :] >= band_low[:, None]) & (bin_index[None, :] < band_high[:, None])).astype(jnp.float32)
    cosine, sine_part = phase_tables(0, LAGS, LAGS, NF)
    norm_factor = 1.0 / math.sqrt(SEGS * NF * DAYS)

    def correlate(pair_row):
        first_block = jnp.maximum(pair_row[0], 0)
        second_block = jnp.maximum(pair_row[1], 0)
        left_block = blocks[:, first_block]
        partner = blocks[:, second_block].astype(jnp.float32)
        joint_keep = keep_mask[first_block] * keep_mask[second_block]
        cos_joint = (cosine * joint_keep)[None, :, None, None, :]
        sin_joint = (sine_part * joint_keep)[None, :, None, None, :]
        real_part = partner[:, None, :, 0]
        imag_part = partner[:, None, :, 1]
        rotated = jnp.stack([real_part * cos_joint + imag_part * sin_joint, imag_part * cos_joint - real_part * sin_joint], axis=3).astype(jnp.bfloat16)
        left_flat = left_block.reshape(DAYS, BLOCK, -1).astype(jnp.float32)
        rotated_flat = rotated.reshape(DAYS, LAGS, BLOCK, -1).astype(jnp.float32)
        output = jnp.einsum('dck,dlnk->lcn', left_flat, rotated_flat) * norm_factor
        return jnp.where(pair_row[0] >= 0, output, jnp.zeros_like(output))
    result = lax.map(correlate, pair_list)
    return jnp.transpose(result, (1, 0, 2, 3))
```

```python
import functools
import math

import jax
import jax.numpy as jnp
from jax import lax
from jax.experimental import pallas as pl
from jax.experimental.pallas import tpu as pltpu
from jax.sharding import PartitionSpec as P

BLK_DEV = 2
SEGLEN = 15000
FIRST = 90
HALF_WIN = 64
LSTEP = 25
REACH = 3
MESH = pl.DeviceIdType.MESH
VMEM = pl.BlockSpec(memory_space=pltpu.VMEM)
SMEM = pl.BlockSpec(memory_space=pltpu.SMEM)


def phase_tables(lag_total, bin_count):
    lag_index = jnp.arange(lag_total, dtype=jnp.int32)
    lag_samples = (lag_index - lag_total // 2) * LSTEP
    bin_number = FIRST + jnp.arange(bin_count, dtype=jnp.int32)
    phase_turns = lag_samples[:, None] * bin_number[None, :] % SEGLEN
    phase_angle = phase_turns.astype(jnp.float32) * (2.0 * math.pi / SEGLEN)
    return jnp.stack([jnp.cos(phase_angle), jnp.sin(phase_angle)], axis=1)


def mixed(index, offset):
    result = index
    bit = 1
    while bit <= offset:
        if offset & bit:
            result = result + bit - 2 * bit * ((index // bit) % 2)
        bit *= 2
    return result


def whiten_kernel(low_ref, high_ref, raw_ref, out_ref, spread_ref):
    bins = raw_ref.shape[-1]

    @pl.when(pl.program_id(0) == 0)
    def _():
        row = lax.broadcasted_iota(jnp.int32, (bins, bins), 0)
        col = lax.broadcasted_iota(jnp.int32, (bins, bins), 1)
        spread_ref[...] = jnp.where(jnp.abs(row - col) <= HALF_WIN, 1.0, 0.0).astype(jnp.bfloat16)

    bin_index = lax.broadcasted_iota(jnp.int32, (1, bins), 1)
    counts = (
        jnp.minimum(bin_index + HALF_WIN, bins - 1) - jnp.maximum(bin_index - HALF_WIN, 0) + 1
    ).astype(jnp.float32)
    spread = spread_ref[...]
    for block in range(BLK_DEV):
        real = raw_ref[0, 0, block].astype(jnp.float32)
        imag = raw_ref[0, 1, block].astype(jnp.float32)
        magnitude = jnp.sqrt(real * real + imag * imag)
        coarse = magnitude.astype(jnp.bfloat16)
        fine = (magnitude - coarse.astype(jnp.float32)).astype(jnp.bfloat16)
        sums = jnp.dot(coarse, spread, preferred_element_type=jnp.float32) + jnp.dot(
            fine, spread, preferred_element_type=jnp.float32
        )
        amplitude = sums / counts + 1e-05
        keep = (bin_index >= low_ref[block]) & (bin_index < high_ref[block])
        gain = 1.0 / amplitude
        out_ref[0, 0, block] = jnp.where(keep, real * gain, 0.0).astype(jnp.bfloat16)
        out_ref[0, 1, block] = jnp.where(keep, imag * gain, 0.0).astype(jnp.bfloat16)


def gather_kernel(
    tiles, group, pair_ref, own_ref, win_ref, gath_ref,
    send_sem, recv_sem, down_send, down_recv, pair_send, pair_recv, own_sem,
):
    here = lax.axis_index("tile")
    spot = here % group
    base = here - spot
    chunks = 2 * BLK_DEV

    barrier = pltpu.get_barrier_semaphore()
    for offset in range(1, group):
        pl.semaphore_signal(
            barrier, inc=1, device_id={"tile": base + mixed(spot, offset)}, device_id_type=MESH
        )

    @pl.when(base > 0)
    def _():
        pl.semaphore_signal(barrier, inc=1, device_id={"tile": here - group}, device_id_type=MESH)

    @pl.when(base + group < tiles)
    def _():
        pl.semaphore_signal(barrier, inc=1, device_id={"tile": here + group}, device_id_type=MESH)

    peers = group - 1 + (base > 0).astype(jnp.int32) + (base + group < tiles).astype(jnp.int32)
    pl.semaphore_wait(barrier, peers)

    def across(offset, chunk):
        part, block = divmod(chunk, BLK_DEV)
        there = mixed(spot, offset)
        return pltpu.make_async_remote_copy(
            src_ref=own_ref.at[there, part, block],
            dst_ref=win_ref.at[spot, part, block],
            send_sem=send_sem.at[offset - 1, chunk],
            recv_sem=recv_sem.at[offset - 1, chunk],
            device_id={"tile": base + there},
            device_id_type=MESH,
        )

    def pairs_across(offset):
        return pltpu.make_async_remote_copy(
            src_ref=pair_ref,
            dst_ref=gath_ref.at[spot],
            send_sem=pair_send.at[offset - 1],
            recv_sem=pair_recv.at[offset - 1],
            device_id={"tile": base + mixed(spot, offset)},
            device_id_type=MESH,
        )

    def down(source, slot, chunk):
        part, block = divmod(chunk, BLK_DEV)
        return pltpu.make_async_remote_copy(
            src_ref=source.at[slot, part, block],
            dst_ref=win_ref.at[group + slot, part, block],
            send_sem=down_send.at[slot, chunk],
            recv_sem=down_recv.at[slot, chunk],
            device_id={"tile": here - group},
            device_id_type=MESH,
        )

    for offset in range(1, group):
        pairs_across(offset).start()
    for chunk in range(chunks):
        for offset in range(1, group):
            across(offset, chunk).start()

    sends_own = (base > 0) & (spot < REACH)

    @pl.when(sends_own)
    def _():
        for chunk in range(chunks):
            down(own_ref, spot, chunk).start()

    stay = pltpu.make_async_copy(own_ref.at[spot], win_ref.at[spot], own_sem)
    stay.start()
    gath_ref[spot] = pair_ref[...]

    for chunk in range(chunks):
        for offset in range(1, group):
            across(offset, chunk).wait_recv()
            there = mixed(spot, offset)

            @pl.when((base > 0) & (there < REACH))
            def _():
                down(win_ref, there, chunk).start()

    for chunk in range(chunks):
        for offset in range(1, group):
            across(offset, chunk).wait_send()
    for offset in range(1, group):
        pairs_across(offset).wait()
    stay.wait()

    @pl.when(base > 0)
    def _():
        for slot in range(REACH):
            for chunk in range(chunks):
                down(win_ref, slot, chunk).wait_send()

    @pl.when(base + group < tiles)
    def _():
        for slot in range(REACH):
            for chunk in range(chunks):
                down(win_ref, slot, chunk).wait_recv()


def pair_kernel(group, lags, rows_dev, norm_factor, pair_ref, trig_ref, win_ref, out_ref, rot_ref):
    base_block = (lax.axis_index("tile") // group) * group * BLK_DEV
    window_tiles, _, _, chans, _ = win_ref.shape

    def rotate(tile, carry):
        for block in range(BLK_DEV):
            real = win_ref[tile, 0, block].astype(jnp.float32)
            imag = win_ref[tile, 1, block].astype(jnp.float32)
            for lag in range(lags):
                cosine = trig_ref[lag, 0:1]
                sine = trig_ref[lag, 1:2]
                rows = slice(lag * chans, (lag + 1) * chans)
                rot_ref[tile * BLK_DEV + block, 0, rows] = (real * cosine + imag * sine).astype(
                    jnp.bfloat16
                )
                rot_ref[tile * BLK_DEV + block, 1, rows] = (imag * cosine - real * sine).astype(
                    jnp.bfloat16
                )
        return carry

    lax.fori_loop(0, window_tiles, rotate, 0)

    def tile_pairs(tile, carry):
        for row in range(rows_dev):
            first = pair_ref[tile, row, 0]
            second = pair_ref[tile, row, 1]
            left = jnp.maximum(first - base_block, 0)
            right = jnp.maximum(second - base_block, 0)
            total = jnp.zeros((chans, lags * chans), jnp.float32)
            for part in range(2):
                total = total + lax.dot_general(
                    win_ref[left // BLK_DEV, part, left % BLK_DEV],
                    rot_ref[right, part],
                    (((1,), (1,)), ((), ())),
                    preferred_element_type=jnp.float32,
                )
            total = jnp.where(first >= 0, total * norm_factor, 0.0)
            for lag in range(lags):
                out_ref[lag, tile, row] = total[:, lag * chans : (lag + 1) * chans]
        return carry

    lax.fori_loop(0, group, tile_pairs, 0)


def reduce_kernel(
    days, group, part_ref, out_ref, day_buf, send_buf, recv_buf,
    day_send, day_recv, tile_send, tile_recv,
):
    here = lax.axis_index("tile")
    day = lax.axis_index("day")
    spot = here % group
    base = here - spot

    barrier = pltpu.get_barrier_semaphore()
    for offset in range(1, days):
        pl.semaphore_signal(
            barrier, inc=1, device_id={"day": (day + offset) % days}, device_id_type=MESH
        )
    for offset in range(1, group):
        pl.semaphore_signal(
            barrier, inc=1, device_id={"tile": base + mixed(spot, offset)}, device_id_type=MESH
        )
    pl.semaphore_wait(barrier, days - 1 + group - 1)

    order = list(range(group - 1, -1, -1))

    def day_copy(step, offset):
        target = (day + step) % days
        there = mixed(spot, offset)
        return pltpu.make_async_remote_copy(
            src_ref=part_ref.at[target, there],
            dst_ref=day_buf.at[step - 1, offset],
            send_sem=day_send.at[step - 1, offset],
            recv_sem=day_recv.at[step - 1, offset],
            device_id={"day": target},
            device_id_type=MESH,
        )

    def tile_copy(offset):
        return pltpu.make_async_remote_copy(
            src_ref=send_buf.at[offset - 1],
            dst_ref=recv_buf.at[offset - 1],
            send_sem=tile_send.at[offset - 1],
            recv_sem=tile_recv.at[offset - 1],
            device_id={"tile": base + mixed(spot, offset)},
            device_id_type=MESH,
        )

    for offset in order:
        for step in range(1, days):
            day_copy(step, offset).start()
    for offset in order:
        total = part_ref[day, mixed(spot, offset)]
        for step in range(1, days):
            day_copy(step, offset).wait_recv()
            total = total + day_buf[step - 1, offset]
        if offset:
            send_buf[offset - 1] = total.astype(jnp.bfloat16)
            tile_copy(offset).start()
        else:
            out_ref[0] = total
    for offset in order[:-1]:
        tile_copy(offset).wait()
        out_ref[0] += recv_buf[offset - 1].astype(jnp.float32)
    for offset in order:
        for step in range(1, days):
            day_copy(step, offset).wait_send()


def per_device(tiles, days, spectra, band_low, band_high, pair_list):
    own = spectra[0]
    channels, parts, segments, bins = own.shape
    group = segments
    chans = channels // BLK_DEV
    rows_dev = pair_list.shape[0]
    lags = days
    norm_factor = 1.0 / math.sqrt(segments * bins * days)
    slice_shape = (parts, BLK_DEV, chans, bins)
    raw = jnp.transpose(own.reshape(BLK_DEV, chans, parts, segments, bins), (3, 2, 0, 1, 4))

    whitened = pl.pallas_call(
        whiten_kernel,
        grid=(segments,),
        out_shape=jax.ShapeDtypeStruct((segments,) + slice_shape, jnp.bfloat16),
        in_specs=[SMEM, SMEM, pl.BlockSpec((1,) + slice_shape, lambda s: (s, 0, 0, 0, 0))],
        out_specs=pl.BlockSpec((1,) + slice_shape, lambda s: (s, 0, 0, 0, 0)),
        scratch_shapes=[pltpu.VMEM((bins, bins), jnp.bfloat16)],
    )(band_low, band_high, raw)

    padded = jnp.pad(pair_list, ((0, 8 - rows_dev), (0, 126)), constant_values=-1)
    chunks = 2 * BLK_DEV
    window, gathered = pl.pallas_call(
        functools.partial(gather_kernel, tiles, group),
        out_shape=[
            jax.ShapeDtypeStruct((group + REACH,) + slice_shape, jnp.bfloat16),
            jax.ShapeDtypeStruct((group,) + padded.shape, jnp.int32),
        ],
        in_specs=[VMEM, VMEM],
        out_specs=[VMEM, VMEM],
        scratch_shapes=[
            pltpu.SemaphoreType.DMA((group - 1, chunks)),
            pltpu.SemaphoreType.DMA((group - 1, chunks)),
            pltpu.SemaphoreType.DMA((REACH, chunks)),
            pltpu.SemaphoreType.DMA((REACH, chunks)),
            pltpu.SemaphoreType.DMA((group - 1,)),
            pltpu.SemaphoreType.DMA((group - 1,)),
            pltpu.SemaphoreType.DMA,
        ],
        compiler_params=pltpu.CompilerParams(collective_id=0, has_side_effects=True),
    )(padded, whitened)

    partial = pl.pallas_call(
        functools.partial(pair_kernel, group, lags, rows_dev, norm_factor),
        out_shape=jax.ShapeDtypeStruct((lags, group, rows_dev, chans, chans), jnp.float32),
        in_specs=[SMEM, VMEM, VMEM],
        out_specs=VMEM,
        scratch_shapes=[
            pltpu.VMEM(((group + REACH) * BLK_DEV, parts, lags * chans, bins), jnp.bfloat16)
        ],
        compiler_params=pltpu.CompilerParams(vmem_limit_bytes=60 * 1024 * 1024),
    )(gathered, phase_tables(lags, bins), window)

    block_shape = (rows_dev, chans, chans)
    return pl.pallas_call(
        functools.partial(reduce_kernel, days, group),
        out_shape=jax.ShapeDtypeStruct((1,) + block_shape, jnp.float32),
        in_specs=[VMEM],
        out_specs=VMEM,
        scratch_shapes=[
            pltpu.VMEM((days - 1, group) + block_shape, jnp.float32),
            pltpu.VMEM((group - 1,) + block_shape, jnp.bfloat16),
            pltpu.VMEM((group - 1,) + block_shape, jnp.bfloat16),
            pltpu.SemaphoreType.DMA((days - 1, group)),
            pltpu.SemaphoreType.DMA((days - 1, group)),
            pltpu.SemaphoreType.DMA((group - 1,)),
            pltpu.SemaphoreType.DMA((group - 1,)),
        ],
        compiler_params=pltpu.CompilerParams(collective_id=1, has_side_effects=True),
    )(partial)


def solution(mesh):
    placed = (P("day", "tile", None, None, None), P("tile"), P("tile"), P("tile", None))
    return jax.shard_map(
        functools.partial(per_device, mesh.shape["tile"], mesh.shape["day"]),
        mesh=mesh,
        in_specs=placed,
        out_specs=P("day", "tile", None, None),
        check_vma=False,
    )
```

```python
import functools
import math

import jax
import jax.numpy as jnp
from jax import lax
from jax.experimental import pallas as pl
from jax.experimental.pallas import tpu as pltpu
from jax.sharding import PartitionSpec as P

BLK_DEV = 2
SEGLEN = 15000
FIRST = 90
HALF_WIN = 64
LSTEP = 25
REACH = 3
BELOW = 1
MESH = pl.DeviceIdType.MESH
VMEM = pl.BlockSpec(memory_space=pltpu.VMEM)
SMEM = pl.BlockSpec(memory_space=pltpu.SMEM)


def phase_tables(lag_total, bin_count):
    lag_index = jnp.arange(lag_total, dtype=jnp.int32)
    lag_samples = (lag_index - lag_total // 2) * LSTEP
    bin_number = FIRST + jnp.arange(bin_count, dtype=jnp.int32)
    phase_turns = lag_samples[:, None] * bin_number[None, :] % SEGLEN
    phase_angle = phase_turns.astype(jnp.float32) * (2.0 * math.pi / SEGLEN)
    return jnp.stack([jnp.cos(phase_angle), jnp.sin(phase_angle)], axis=1)


def mixed(index, offset):
    result = index
    bit = 1
    while bit <= offset:
        if offset & bit:
            result = result + bit - 2 * bit * ((index // bit) % 2)
        bit *= 2
    return result


def whiten_kernel(low_ref, high_ref, raw_ref, out_ref, spread_ref):
    bins = raw_ref.shape[-1]

    @pl.when(pl.program_id(0) == 0)
    def _():
        row = lax.broadcasted_iota(jnp.int32, (bins, bins), 0)
        col = lax.broadcasted_iota(jnp.int32, (bins, bins), 1)
        spread_ref[...] = jnp.where(jnp.abs(row - col) <= HALF_WIN, 1.0, 0.0).astype(jnp.bfloat16)

    bin_index = lax.broadcasted_iota(jnp.int32, (1, bins), 1)
    counts = (
        jnp.minimum(bin_index + HALF_WIN, bins - 1) - jnp.maximum(bin_index - HALF_WIN, 0) + 1
    ).astype(jnp.float32)
    spread = spread_ref[...]
    for block in range(BLK_DEV):
        real = raw_ref[0, 0, block].astype(jnp.float32)
        imag = raw_ref[0, 1, block].astype(jnp.float32)
        magnitude = jnp.sqrt(real * real + imag * imag)
        coarse = magnitude.astype(jnp.bfloat16)
        fine = (magnitude - coarse.astype(jnp.float32)).astype(jnp.bfloat16)
        sums = jnp.dot(coarse, spread, preferred_element_type=jnp.float32) + jnp.dot(
            fine, spread, preferred_element_type=jnp.float32
        )
        amplitude = sums / counts + 1e-05
        keep = (bin_index >= low_ref[block]) & (bin_index < high_ref[block])
        gain = 1.0 / amplitude
        out_ref[0, 0, block] = jnp.where(keep, real * gain, 0.0).astype(jnp.bfloat16)
        out_ref[0, 1, block] = jnp.where(keep, imag * gain, 0.0).astype(jnp.bfloat16)


def gather_kernel(
    tiles, group, pair_ref, own_ref, win_ref, gath_ref,
    send_sem, recv_sem, far_send, far_recv, pair_send, pair_recv, up_send, up_recv, own_sem,
):
    here = lax.axis_index("tile")
    spot = here % group
    base = here - spot
    chunks = 2 * BLK_DEV
    has_below = base > 0
    has_above = base + group < tiles
    upper = REACH - BELOW

    barrier = pltpu.get_barrier_semaphore()
    for offset in range(1, group):
        pl.semaphore_signal(
            barrier, inc=1, device_id={"tile": base + mixed(spot, offset)}, device_id_type=MESH
        )

    @pl.when(has_below)
    def _():
        pl.semaphore_signal(barrier, inc=1, device_id={"tile": here - group}, device_id_type=MESH)

    @pl.when(has_above)
    def _():
        pl.semaphore_signal(barrier, inc=1, device_id={"tile": here + group}, device_id_type=MESH)

    peers = group - 1 + has_below.astype(jnp.int32) + has_above.astype(jnp.int32)
    pl.semaphore_wait(barrier, peers)

    def across(offset, chunk):
        part, block = divmod(chunk, BLK_DEV)
        there = mixed(spot, offset)
        return pltpu.make_async_remote_copy(
            src_ref=own_ref.at[there, part, block],
            dst_ref=win_ref.at[BELOW + spot, part, block],
            send_sem=send_sem.at[offset - 1, chunk],
            recv_sem=recv_sem.at[offset - 1, chunk],
            device_id={"tile": base + there},
            device_id_type=MESH,
        )

    def pairs_across(offset):
        return pltpu.make_async_remote_copy(
            src_ref=pair_ref,
            dst_ref=gath_ref.at[BELOW + spot],
            send_sem=pair_send.at[offset - 1],
            recv_sem=pair_recv.at[offset - 1],
            device_id={"tile": base + mixed(spot, offset)},
            device_id_type=MESH,
        )

    def pairs_up():
        return pltpu.make_async_remote_copy(
            src_ref=gath_ref.at[group],
            dst_ref=gath_ref.at[0],
            send_sem=up_send,
            recv_sem=up_recv,
            device_id={"tile": here + group},
            device_id_type=MESH,
        )

    def far(source, slot, target, device, chunk):
        part, block = divmod(chunk, BLK_DEV)
        index = 0 if target == 0 else target - BELOW - group + 1
        return pltpu.make_async_remote_copy(
            src_ref=source.at[slot, part, block],
            dst_ref=win_ref.at[target, part, block],
            send_sem=far_send.at[index, chunk],
            recv_sem=far_recv.at[index, chunk],
            device_id={"tile": device},
            device_id_type=MESH,
        )

    def relay(source, slot, where, chunk_list):
        for lower in range(upper):

            @pl.when(has_below & (where == lower))
            def _():
                for chunk in chunk_list:
                    far(source, slot, BELOW + group + lower, here - group, chunk).start()

        @pl.when(has_above & (where == group - 1))
        def _():
            for chunk in chunk_list:
                far(source, slot, 0, here + group, chunk).start()

    for offset in range(1, group):
        pairs_across(offset).start()
    for chunk in range(chunks):
        for offset in range(1, group):
            across(offset, chunk).start()
    relay(own_ref, spot, spot, range(chunks))
    stay = pltpu.make_async_copy(own_ref.at[spot], win_ref.at[BELOW + spot], own_sem)
    stay.start()
    gath_ref[BELOW + spot] = pair_ref[...]

    for chunk in range(chunks):
        for offset in range(1, group):
            across(offset, chunk).wait_recv()
            there = mixed(spot, offset)
            relay(win_ref, BELOW + there, there, [chunk])

    for chunk in range(chunks):
        for offset in range(1, group):
            across(offset, chunk).wait_send()
    stay.wait()
    for offset in range(1, group):
        pairs_across(offset).wait()

    @pl.when(has_above)
    def _():
        pairs_up().start()
        pairs_up().wait_send()
        for chunk in range(chunks):
            far(own_ref, 0, 0, here + group, chunk).wait_send()
            for lower in range(upper):
                far(own_ref, 0, BELOW + group + lower, here, chunk).wait_recv()

    @pl.when(has_below)
    def _():
        pairs_up().wait_recv()
        for chunk in range(chunks):
            far(own_ref, 0, 0, here, chunk).wait_recv()
            for lower in range(upper):
                far(own_ref, 0, BELOW + group + lower, here - group, chunk).wait_send()

    @pl.when(base == 0)
    def _():
        gath_ref[0] = jnp.full(pair_ref.shape, -1, jnp.int32)


def pair_kernel(
    tiles, days, group, norm_factor, pair_ref, trig_ref, win_ref, out_ref,
    rot_ref, part_ref, day_buf, send_buf, recv_buf, top_buf, down_src, down_buf,
    day_send, day_recv, tile_send, tile_recv, top_send, top_recv, down_send, down_recv,
):
    here = lax.axis_index("tile")
    day = lax.axis_index("day")
    spot = here % group
    base = here - spot
    last = group - 1
    has_below = base > 0
    has_above = base + group < tiles
    is_top = base + group == tiles
    base_block = (base - BELOW) * BLK_DEV
    window_tiles, _, _, chans, _ = win_ref.shape
    lags = days
    rows_dev = out_ref.shape[1]

    barrier = pltpu.get_barrier_semaphore()
    for offset in range(1, days):
        pl.semaphore_signal(
            barrier, inc=1, device_id={"day": (day + offset) % days}, device_id_type=MESH
        )
    for offset in range(1, group):
        pl.semaphore_signal(
            barrier, inc=1, device_id={"tile": base + mixed(spot, offset)}, device_id_type=MESH
        )

    @pl.when(has_below)
    def _():
        pl.semaphore_signal(barrier, inc=1, device_id={"tile": here - group}, device_id_type=MESH)

    @pl.when(has_above)
    def _():
        pl.semaphore_signal(barrier, inc=1, device_id={"tile": here + group}, device_id_type=MESH)

    def rotate(tile, carry):
        for block in range(BLK_DEV):
            real = win_ref[tile, 0, block].astype(jnp.float32)
            imag = win_ref[tile, 1, block].astype(jnp.float32)
            for lag in range(lags):
                cosine = trig_ref[lag, 0:1]
                sine = trig_ref[lag, 1:2]
                rows = slice(lag * chans, (lag + 1) * chans)
                rot_ref[tile * BLK_DEV + block, 0, rows] = (real * cosine + imag * sine).astype(
                    jnp.bfloat16
                )
                rot_ref[tile * BLK_DEV + block, 1, rows] = (imag * cosine - real * sine).astype(
                    jnp.bfloat16
                )
        return carry

    lax.fori_loop(0, window_tiles, rotate, 0)
    peers = days - 1 + last + has_below.astype(jnp.int32) + has_above.astype(jnp.int32)
    pl.semaphore_wait(barrier, peers)

    def products(set_index, slot):
        for row in range(rows_dev):
            first = pair_ref[set_index, row, 0]
            second = pair_ref[set_index, row, 1]
            left = jnp.clip(first - base_block, 0, window_tiles * BLK_DEV - 1)
            right = jnp.clip(second - base_block, 0, window_tiles * BLK_DEV - 1)
            total = jnp.zeros((chans, lags * chans), jnp.float32)
            for part in range(2):
                total = total + lax.dot_general(
                    win_ref[left // BLK_DEV, part, left % BLK_DEV],
                    rot_ref[right, part],
                    (((1,), (1,)), ((), ())),
                    preferred_element_type=jnp.float32,
                )
            total = jnp.where(first >= 0, total * norm_factor, 0.0)
            for lag in range(lags):
                part_ref[slot, lag, row] = total[:, lag * chans : (lag + 1) * chans]

    def day_copy(step, slot):
        target = (day + step) % days
        return pltpu.make_async_remote_copy(
            src_ref=part_ref.at[slot, target],
            dst_ref=day_buf.at[step - 1, slot],
            send_sem=day_send.at[step - 1, slot],
            recv_sem=day_recv.at[step - 1, slot],
            device_id={"day": target},
            device_id_type=MESH,
        )

    def day_total(slot):
        total = part_ref[slot, day]
        for step in range(1, days):
            day_copy(step, slot).wait_recv()
            total = total + day_buf[step - 1, slot]
        return total

    def tile_copy(offset):
        return pltpu.make_async_remote_copy(
            src_ref=send_buf.at[offset - 1],
            dst_ref=recv_buf.at[offset - 1],
            send_sem=tile_send.at[offset - 1],
            recv_sem=tile_recv.at[offset - 1],
            device_id={"tile": base + mixed(spot, offset)},
            device_id_type=MESH,
        )

    def top_copy(device, slot):
        return pltpu.make_async_remote_copy(
            src_ref=send_buf.at[last],
            dst_ref=top_buf.at[slot],
            send_sem=top_send,
            recv_sem=top_recv.at[slot],
            device_id={"tile": device},
            device_id_type=MESH,
        )

    def down_copy(row, device):
        return pltpu.make_async_remote_copy(
            src_ref=down_src.at[row],
            dst_ref=down_buf.at[row],
            send_sem=down_send.at[row],
            recv_sem=down_recv.at[row],
            device_id={"tile": device},
            device_id_type=MESH,
        )

    def push(offset):
        send_buf[offset - 1] = day_total(offset).astype(jnp.bfloat16)
        tile_copy(offset).start()

    for offset in range(last, -1, -1):
        products((mixed(spot, offset) + BELOW) % group, offset)
        for step in range(1, days):
            day_copy(step, offset).start()
        if offset < last:
            push(offset + 1)

    @pl.when(is_top)
    def _():
        products(group, group)
        for step in range(1, days):
            day_copy(step, group).start()

    out_ref[0] = day_total(0)

    @pl.when(is_top)
    def _():
        total = day_total(group)

        @pl.when(spot < last)
        def _():
            send_buf[last] = total.astype(jnp.bfloat16)
            top_copy(base + last, spot).start()

        @pl.when(spot == last)
        def _():
            down_buf[...] = total

    for offset in range(last, 0, -1):
        tile_copy(offset).wait_recv()
    sends_down = has_below & (spot == last)
    takes_down = has_above & (spot == last)
    for row in range(rows_dev):
        total = out_ref[0, row]
        for offset in range(last, 0, -1):
            total = total + recv_buf[offset - 1, row].astype(jnp.float32)
        out_ref[0, row] = total

        @pl.when(sends_down)
        def _():
            down_src[row] = total
            down_copy(row, here - group).start()

    @pl.when(takes_down)
    def _():
        for row in range(rows_dev):
            down_copy(row, here).wait_recv()
            out_ref[0, row] = down_buf[row]

    @pl.when(is_top & (spot == last))
    def _():
        total = down_buf[...]
        for slot in range(last):
            top_copy(here, slot).wait_recv()
            total = total + top_buf[slot].astype(jnp.float32)
        out_ref[0] = total

    @pl.when(is_top & (spot < last))
    def _():
        top_copy(base + last, spot).wait_send()

    @pl.when(sends_down)
    def _():
        for row in range(rows_dev):
            down_copy(row, here - group).wait_send()

    for offset in range(last, 0, -1):
        tile_copy(offset).wait_send()
    for offset in range(last, -1, -1):
        for step in range(1, days):
            day_copy(step, offset).wait_send()

    @pl.when(is_top)
    def _():
        for step in range(1, days):
            day_copy(step, group).wait_send()


def per_device(tiles, days, spectra, band_low, band_high, pair_list):
    own = spectra[0]
    channels, parts, segments, bins = own.shape
    group = segments
    chans = channels // BLK_DEV
    rows_dev = pair_list.shape[0]
    lags = days
    norm_factor = 1.0 / math.sqrt(segments * bins * days)
    slice_shape = (parts, BLK_DEV, chans, bins)
    raw = jnp.transpose(own.reshape(BLK_DEV, chans, parts, segments, bins), (3, 2, 0, 1, 4))

    whitened = pl.pallas_call(
        whiten_kernel,
        grid=(segments,),
        out_shape=jax.ShapeDtypeStruct((segments,) + slice_shape, jnp.bfloat16),
        in_specs=[SMEM, SMEM, pl.BlockSpec((1,) + slice_shape, lambda s: (s, 0, 0, 0, 0))],
        out_specs=pl.BlockSpec((1,) + slice_shape, lambda s: (s, 0, 0, 0, 0)),
        scratch_shapes=[pltpu.VMEM((bins, bins), jnp.bfloat16)],
    )(band_low, band_high, raw)

    padded = jnp.pad(pair_list, ((0, 8 - rows_dev), (0, 126)), constant_values=-1)
    chunks = 2 * BLK_DEV
    window, gathered = pl.pallas_call(
        functools.partial(gather_kernel, tiles, group),
        out_shape=[
            jax.ShapeDtypeStruct((group + REACH,) + slice_shape, jnp.bfloat16),
            jax.ShapeDtypeStruct((BELOW + group,) + padded.shape, jnp.int32),
        ],
        in_specs=[VMEM, VMEM],
        out_specs=[VMEM, VMEM],
        scratch_shapes=[
            pltpu.SemaphoreType.DMA((group - 1, chunks)),
            pltpu.SemaphoreType.DMA((group - 1, chunks)),
            pltpu.SemaphoreType.DMA((REACH, chunks)),
            pltpu.SemaphoreType.DMA((REACH, chunks)),
            pltpu.SemaphoreType.DMA((group - 1,)),
            pltpu.SemaphoreType.DMA((group - 1,)),
            pltpu.SemaphoreType.DMA,
            pltpu.SemaphoreType.DMA,
            pltpu.SemaphoreType.DMA,
        ],
        compiler_params=pltpu.CompilerParams(collective_id=0, has_side_effects=True),
    )(padded, whitened)

    block_shape = (rows_dev, chans, chans)
    return pl.pallas_call(
        functools.partial(pair_kernel, tiles, days, group, norm_factor),
        out_shape=jax.ShapeDtypeStruct((1,) + block_shape, jnp.float32),
        in_specs=[SMEM, VMEM, VMEM],
        out_specs=VMEM,
        scratch_shapes=[
            pltpu.VMEM(((group + REACH) * BLK_DEV, parts, lags * chans, bins), jnp.bfloat16),
            pltpu.VMEM((group + 1, lags) + block_shape, jnp.float32),
            pltpu.VMEM((days - 1, group + 1) + block_shape, jnp.float32),
            pltpu.VMEM((group,) + block_shape, jnp.bfloat16),
            pltpu.VMEM((group - 1,) + block_shape, jnp.bfloat16),
            pltpu.VMEM((group - 1,) + block_shape, jnp.bfloat16),
            pltpu.VMEM(block_shape, jnp.float32),
            pltpu.VMEM(block_shape, jnp.float32),
            pltpu.SemaphoreType.DMA((days - 1, group + 1)),
            pltpu.SemaphoreType.DMA((days - 1, group + 1)),
            pltpu.SemaphoreType.DMA((group - 1,)),
            pltpu.SemaphoreType.DMA((group - 1,)),
            pltpu.SemaphoreType.DMA,
            pltpu.SemaphoreType.DMA((group - 1,)),
            pltpu.SemaphoreType.DMA((rows_dev,)),
            pltpu.SemaphoreType.DMA((rows_dev,)),
        ],
        compiler_params=pltpu.CompilerParams(
            collective_id=1, has_side_effects=True, vmem_limit_bytes=63 * 1024 * 1024
        ),
    )(gathered, phase_tables(lags, bins), window)


def solution(mesh):
    placed = (P("day", "tile", None, None, None), P("tile"), P("tile"), P("tile", None))
    return jax.shard_map(
        functools.partial(per_device, mesh.shape["tile"], mesh.shape["day"]),
        mesh=mesh,
        in_specs=placed,
        out_specs=P("day", "tile", None, None),
        check_vma=False,
    )
```

```python
import functools
import math

import jax
import jax.numpy as jnp
import numpy as np
from jax import lax
from jax.experimental import pallas as pl
from jax.experimental.pallas import tpu as pltpu
from jax.sharding import PartitionSpec as P

BLK_DEV = 2
SEGLEN = 15000
FIRST = 90
HALF_WIN = 64
LSTEP = 25
REACH = 3
BELOW = 1
MESH = pl.DeviceIdType.MESH
VMEM = pl.BlockSpec(memory_space=pltpu.VMEM)
SMEM = pl.BlockSpec(memory_space=pltpu.SMEM)


def phase_tables(lag_total, bin_count):
    lag_samples = (np.arange(lag_total) - lag_total // 2) * LSTEP
    bin_number = FIRST + np.arange(bin_count)
    phase_turns = lag_samples[:, None] * bin_number[None, :] % SEGLEN
    phase_angle = phase_turns.astype(np.float32) * np.float32(2.0 * math.pi / SEGLEN)
    return np.stack([np.cos(phase_angle), np.sin(phase_angle)], axis=1).astype(np.float32)


def mixed(index, offset):
    result = index
    bit = 1
    while bit <= offset:
        if offset & bit:
            result = result + bit - 2 * bit * ((index // bit) % 2)
        bit *= 2
    return result


def whiten_kernel(low_ref, high_ref, pair_ref, raw_ref, out_ref, padded_ref, spread_ref):
    bins = raw_ref.shape[-1]

    @pl.when(pl.program_id(0) == 0)
    def _():
        row = lax.broadcasted_iota(jnp.int32, (bins, bins), 0)
        col = lax.broadcasted_iota(jnp.int32, (bins, bins), 1)
        spread_ref[...] = jnp.where(jnp.abs(row - col) <= HALF_WIN, 1.0, 0.0).astype(jnp.bfloat16)
        row = lax.broadcasted_iota(jnp.int32, padded_ref.shape, 0)
        col = lax.broadcasted_iota(jnp.int32, padded_ref.shape, 1)
        padded = jnp.full(padded_ref.shape, -1, jnp.int32)
        for pair in range(pair_ref.shape[0]):
            for side in range(2):
                padded = jnp.where((row == pair) & (col == side), pair_ref[pair, side], padded)
        padded_ref[...] = padded

    bin_index = lax.broadcasted_iota(jnp.int32, (1, bins), 1)
    counts = (
        jnp.minimum(bin_index + HALF_WIN, bins - 1) - jnp.maximum(bin_index - HALF_WIN, 0) + 1
    ).astype(jnp.float32)
    spread = spread_ref[...]
    for block in range(BLK_DEV):
        real = raw_ref[0, 0, block].astype(jnp.float32)
        imag = raw_ref[0, 1, block].astype(jnp.float32)
        magnitude = jnp.sqrt(real * real + imag * imag)
        coarse = magnitude.astype(jnp.bfloat16)
        fine = (magnitude - coarse.astype(jnp.float32)).astype(jnp.bfloat16)
        sums = jnp.dot(coarse, spread, preferred_element_type=jnp.float32) + jnp.dot(
            fine, spread, preferred_element_type=jnp.float32
        )
        amplitude = sums / counts + 1e-05
        keep = (bin_index >= low_ref[block]) & (bin_index < high_ref[block])
        gain = 1.0 / amplitude
        out_ref[0, 0, block] = jnp.where(keep, real * gain, 0.0).astype(jnp.bfloat16)
        out_ref[0, 1, block] = jnp.where(keep, imag * gain, 0.0).astype(jnp.bfloat16)


def correlate_kernel(
    tiles, days, group, norm_factor, own_pair_ref, trig_ref, own_ref, out_ref,
    win_ref, gath_ref, pair_ref,
    rot_ref, part_ref, day_buf, send_buf, recv_buf, top_buf, down_src, down_buf,
    send_sem, recv_sem, far_send, far_recv, pair_send, pair_recv, up_send, up_recv, own_sem,
    day_send, day_recv, tile_send, tile_recv, top_send, top_recv, down_send, down_recv,
):
    here = lax.axis_index("tile")
    day = lax.axis_index("day")
    spot = here % group
    base = here - spot
    chunks = 2 * BLK_DEV
    has_below = base > 0
    has_above = base + group < tiles
    upper = REACH - BELOW

    last = group - 1
    is_top = base + group == tiles
    base_block = (base - BELOW) * BLK_DEV
    window_tiles, _, _, chans, _ = win_ref.shape
    lags = days
    rows_dev = out_ref.shape[1]

    barrier = pltpu.get_barrier_semaphore()
    for offset in range(1, days):
        pl.semaphore_signal(
            barrier, inc=1, device_id={"day": (day + offset) % days}, device_id_type=MESH
        )
    for offset in range(1, group):
        pl.semaphore_signal(
            barrier, inc=1, device_id={"tile": base + mixed(spot, offset)}, device_id_type=MESH
        )

    @pl.when(has_below)
    def _():
        pl.semaphore_signal(barrier, inc=1, device_id={"tile": here - group}, device_id_type=MESH)

    @pl.when(has_above)
    def _():
        pl.semaphore_signal(barrier, inc=1, device_id={"tile": here + group}, device_id_type=MESH)

    peers = days - 1 + group - 1 + has_below.astype(jnp.int32) + has_above.astype(jnp.int32)
    pl.semaphore_wait(barrier, peers)

    def across(offset, chunk):
        block, part = divmod(chunk, 2)
        there = mixed(spot, offset)
        return pltpu.make_async_remote_copy(
            src_ref=own_ref.at[there, part, block],
            dst_ref=win_ref.at[BELOW + spot, part, block],
            send_sem=send_sem.at[offset - 1, chunk],
            recv_sem=recv_sem.at[offset - 1, chunk],
            device_id={"tile": base + there},
            device_id_type=MESH,
        )

    def pairs_across(offset):
        return pltpu.make_async_remote_copy(
            src_ref=own_pair_ref,
            dst_ref=gath_ref.at[BELOW + spot],
            send_sem=pair_send.at[offset - 1],
            recv_sem=pair_recv.at[offset - 1],
            device_id={"tile": base + mixed(spot, offset)},
            device_id_type=MESH,
        )

    def pairs_up():
        return pltpu.make_async_remote_copy(
            src_ref=gath_ref.at[group],
            dst_ref=gath_ref.at[0],
            send_sem=up_send,
            recv_sem=up_recv,
            device_id={"tile": here + group},
            device_id_type=MESH,
        )

    def far(source, slot, target, device, chunk):
        block, part = divmod(chunk, 2)
        index = 0 if target == 0 else target - BELOW - group + 1
        return pltpu.make_async_remote_copy(
            src_ref=source.at[slot, part, block],
            dst_ref=win_ref.at[target, part, block],
            send_sem=far_send.at[index, chunk],
            recv_sem=far_recv.at[index, chunk],
            device_id={"tile": device},
            device_id_type=MESH,
        )

    def relay(source, slot, where, chunk_list):
        for lower in range(upper):

            @pl.when(has_below & (where == lower))
            def _():
                for chunk in chunk_list:
                    far(source, slot, BELOW + group + lower, here - group, chunk).start()

        @pl.when(has_above & (where == group - 1))
        def _():
            for chunk in chunk_list:
                far(source, slot, 0, here + group, chunk).start()

    for offset in range(1, group):
        pairs_across(offset).start()
    for chunk in range(chunks):
        for offset in range(1, group):
            across(offset, chunk).start()
    relay(own_ref, spot, spot, range(chunks))
    stay = pltpu.make_async_copy(own_ref.at[spot], win_ref.at[BELOW + spot], own_sem)
    stay.start()
    gath_ref[BELOW + spot] = own_pair_ref[...]

    @pl.when(base == 0)
    def _():
        gath_ref[0] = jnp.full(own_pair_ref.shape, -1, jnp.int32)

    for chunk in range(chunks):
        for offset in range(1, group):
            across(offset, chunk).wait_recv()
            there = mixed(spot, offset)
            relay(win_ref, BELOW + there, there, [chunk])

    def rotate(tile, carry):
        for block in range(BLK_DEV):
            real = win_ref[tile, 0, block].astype(jnp.float32)
            imag = win_ref[tile, 1, block].astype(jnp.float32)
            for lag in range(lags):
                cosine = trig_ref[lag, 0:1]
                sine = trig_ref[lag, 1:2]
                rows = slice(lag * chans, (lag + 1) * chans)
                rot_ref[tile * BLK_DEV + block, 0, rows] = (real * cosine + imag * sine).astype(
                    jnp.bfloat16
                )
                rot_ref[tile * BLK_DEV + block, 1, rows] = (imag * cosine - real * sine).astype(
                    jnp.bfloat16
                )
        return carry

    for chunk in range(chunks):
        for offset in range(1, group):
            across(offset, chunk).wait_send()
    stay.wait()
    for offset in range(1, group):
        pairs_across(offset).wait()

    @pl.when(has_above)
    def _():
        pairs_up().start()

    lax.fori_loop(BELOW, BELOW + group, rotate, 0)

    @pl.when(has_above)
    def _():
        pairs_up().wait_send()
        for chunk in range(chunks):
            far(own_ref, 0, 0, here + group, chunk).wait_send()
            for lower in range(upper):
                far(own_ref, 0, BELOW + group + lower, here, chunk).wait_recv()

    @pl.when(has_below)
    def _():
        pairs_up().wait_recv()
        for chunk in range(chunks):
            far(own_ref, 0, 0, here, chunk).wait_recv()
            for lower in range(upper):
                far(own_ref, 0, BELOW + group + lower, here - group, chunk).wait_send()

    gather_pairs = pltpu.make_async_copy(gath_ref, pair_ref, own_sem)
    gather_pairs.start()
    lax.fori_loop(0, BELOW, rotate, 0)
    lax.fori_loop(BELOW + group, window_tiles, rotate, 0)
    gather_pairs.wait()

    def products(set_index, slot):
        for row in range(rows_dev):
            first = pair_ref[set_index, row, 0]
            second = pair_ref[set_index, row, 1]
            left = jnp.clip(first - base_block, 0, window_tiles * BLK_DEV - 1)
            right = jnp.clip(second - base_block, 0, window_tiles * BLK_DEV - 1)
            total = jnp.zeros((chans, lags * chans), jnp.float32)
            for part in range(2):
                total = total + lax.dot_general(
                    win_ref[left // BLK_DEV, part, left % BLK_DEV],
                    rot_ref[right, part],
                    (((1,), (1,)), ((), ())),
                    preferred_element_type=jnp.float32,
                )
            total = jnp.where(first >= 0, total * norm_factor, 0.0)
            for lag in range(lags):
                part_ref[slot, lag, row] = total[:, lag * chans : (lag + 1) * chans]

    def day_copy(step, slot):
        target = (day + step) % days
        return pltpu.make_async_remote_copy(
            src_ref=part_ref.at[slot, target],
            dst_ref=day_buf.at[step - 1, slot],
            send_sem=day_send.at[step - 1, slot],
            recv_sem=day_recv.at[step - 1, slot],
            device_id={"day": target},
            device_id_type=MESH,
        )

    def day_total(slot):
        total = part_ref[slot, day]
        for step in range(1, days):
            day_copy(step, slot).wait_recv()
            total = total + day_buf[step - 1, slot]
        return total

    def tile_copy(offset):
        return pltpu.make_async_remote_copy(
            src_ref=send_buf.at[offset - 1],
            dst_ref=recv_buf.at[offset - 1],
            send_sem=tile_send.at[offset - 1],
            recv_sem=tile_recv.at[offset - 1],
            device_id={"tile": base + mixed(spot, offset)},
            device_id_type=MESH,
        )

    def top_copy(device, slot):
        return pltpu.make_async_remote_copy(
            src_ref=send_buf.at[last],
            dst_ref=top_buf.at[slot],
            send_sem=top_send,
            recv_sem=top_recv.at[slot],
            device_id={"tile": device},
            device_id_type=MESH,
        )

    def down_copy(row, device):
        return pltpu.make_async_remote_copy(
            src_ref=down_src.at[row],
            dst_ref=down_buf.at[row],
            send_sem=down_send.at[row],
            recv_sem=down_recv.at[row],
            device_id={"tile": device},
            device_id_type=MESH,
        )

    def push(offset):
        send_buf[offset - 1] = day_total(offset).astype(jnp.bfloat16)
        tile_copy(offset).start()

    for offset in range(last, -1, -1):
        products((mixed(spot, offset) + BELOW) % group, offset)
        for step in range(1, days):
            day_copy(step, offset).start()
        if offset < last:
            push(offset + 1)

    @pl.when(is_top)
    def _():
        products(group, group)
        for step in range(1, days):
            day_copy(step, group).start()

    out_ref[0] = day_total(0)

    @pl.when(is_top)
    def _():
        total = day_total(group)

        @pl.when(spot < last)
        def _():
            send_buf[last] = total.astype(jnp.bfloat16)
            top_copy(base + last, spot).start()

        @pl.when(spot == last)
        def _():
            down_buf[...] = total

    for offset in range(last, 0, -1):
        tile_copy(offset).wait_recv()
    sends_down = has_below & (spot == last)
    takes_down = has_above & (spot == last)
    for row in range(rows_dev):
        total = out_ref[0, row]
        for offset in range(last, 0, -1):
            total = total + recv_buf[offset - 1, row].astype(jnp.float32)
        out_ref[0, row] = total

        @pl.when(sends_down)
        def _():
            down_src[row] = total
            down_copy(row, here - group).start()

    @pl.when(takes_down)
    def _():
        for row in range(rows_dev):
            down_copy(row, here).wait_recv()
            out_ref[0, row] = down_buf[row]

    @pl.when(is_top & (spot == last))
    def _():
        total = down_buf[...]
        for slot in range(last):
            top_copy(here, slot).wait_recv()
            total = total + top_buf[slot].astype(jnp.float32)
        out_ref[0] = total

    @pl.when(is_top & (spot < last))
    def _():
        top_copy(base + last, spot).wait_send()

    @pl.when(sends_down)
    def _():
        for row in range(rows_dev):
            down_copy(row, here - group).wait_send()

    for offset in range(last, 0, -1):
        tile_copy(offset).wait_send()
    for offset in range(last, -1, -1):
        for step in range(1, days):
            day_copy(step, offset).wait_send()

    @pl.when(is_top)
    def _():
        for step in range(1, days):
            day_copy(step, group).wait_send()


def per_device(tiles, days, spectra, band_low, band_high, pair_list):
    own = spectra[0]
    channels, parts, segments, bins = own.shape
    group = segments
    chans = channels // BLK_DEV
    rows_dev = pair_list.shape[0]
    lags = days
    norm_factor = 1.0 / math.sqrt(segments * bins * days)
    slice_shape = (parts, BLK_DEV, chans, bins)
    raw = jnp.transpose(own.reshape(BLK_DEV, chans, parts, segments, bins), (3, 2, 0, 1, 4))

    whitened, padded = pl.pallas_call(
        whiten_kernel,
        grid=(segments,),
        out_shape=[
            jax.ShapeDtypeStruct((segments,) + slice_shape, jnp.bfloat16),
            jax.ShapeDtypeStruct((8, 128), jnp.int32),
        ],
        in_specs=[SMEM, SMEM, SMEM, pl.BlockSpec((1,) + slice_shape, lambda s: (s, 0, 0, 0, 0))],
        out_specs=[
            pl.BlockSpec((1,) + slice_shape, lambda s: (s, 0, 0, 0, 0)),
            pl.BlockSpec((8, 128), lambda s: (0, 0)),
        ],
        scratch_shapes=[pltpu.VMEM((bins, bins), jnp.bfloat16)],
    )(band_low, band_high, pair_list, raw)

    chunks = 2 * BLK_DEV
    block_shape = (rows_dev, chans, chans)
    gathered_shape = (BELOW + group, 8, 128)
    return pl.pallas_call(
        functools.partial(correlate_kernel, tiles, days, group, norm_factor),
        out_shape=jax.ShapeDtypeStruct((1,) + block_shape, jnp.float32),
        in_specs=[VMEM, VMEM, VMEM],
        out_specs=VMEM,
        scratch_shapes=[
            pltpu.VMEM((group + REACH,) + slice_shape, jnp.bfloat16),
            pltpu.VMEM(gathered_shape, jnp.int32),
            pltpu.SMEM(gathered_shape, jnp.int32),
            pltpu.VMEM(((group + REACH) * BLK_DEV, parts, lags * chans, bins), jnp.bfloat16),
            pltpu.VMEM((group + 1, lags) + block_shape, jnp.float32),
            pltpu.VMEM((days - 1, group + 1) + block_shape, jnp.float32),
            pltpu.VMEM((group,) + block_shape, jnp.bfloat16),
            pltpu.VMEM((group - 1,) + block_shape, jnp.bfloat16),
            pltpu.VMEM((group - 1,) + block_shape, jnp.bfloat16),
            pltpu.VMEM(block_shape, jnp.float32),
            pltpu.VMEM(block_shape, jnp.float32),
            pltpu.SemaphoreType.DMA((group - 1, chunks)),
            pltpu.SemaphoreType.DMA((group - 1, chunks)),
            pltpu.SemaphoreType.DMA((REACH, chunks)),
            pltpu.SemaphoreType.DMA((REACH, chunks)),
            pltpu.SemaphoreType.DMA((group - 1,)),
            pltpu.SemaphoreType.DMA((group - 1,)),
            pltpu.SemaphoreType.DMA,
            pltpu.SemaphoreType.DMA,
            pltpu.SemaphoreType.DMA,
            pltpu.SemaphoreType.DMA((days - 1, group + 1)),
            pltpu.SemaphoreType.DMA((days - 1, group + 1)),
            pltpu.SemaphoreType.DMA((group - 1,)),
            pltpu.SemaphoreType.DMA((group - 1,)),
            pltpu.SemaphoreType.DMA,
            pltpu.SemaphoreType.DMA((group - 1,)),
            pltpu.SemaphoreType.DMA((rows_dev,)),
            pltpu.SemaphoreType.DMA((rows_dev,)),
        ],
        compiler_params=pltpu.CompilerParams(
            collective_id=0, has_side_effects=True, vmem_limit_bytes=63 * 1024 * 1024
        ),
    )(padded, jnp.asarray(phase_tables(lags, bins)), whitened)


def solution(mesh):
    placed = (P("day", "tile", None, None, None), P("tile"), P("tile"), P("tile", None))
    return jax.shard_map(
        functools.partial(per_device, mesh.shape["tile"], mesh.shape["day"]),
        mesh=mesh,
        in_specs=placed,
        out_specs=P("day", "tile", None, None),
        check_vma=False,
    )
```

```python
import functools
import math

import jax
import jax.numpy as jnp
import numpy as np
from jax import lax
from jax.experimental import pallas as pl
from jax.experimental.pallas import tpu as pltpu
from jax.sharding import PartitionSpec as P

BLK_DEV = 2
SEGLEN = 15000
FIRST = 90
HALF_WIN = 64
LSTEP = 25
REACH = 3
BELOW = 1
MESH = pl.DeviceIdType.MESH
VMEM = pl.BlockSpec(memory_space=pltpu.VMEM)
SMEM = pl.BlockSpec(memory_space=pltpu.SMEM)


def phase_tables(lag_total, bin_count):
    lag_samples = (np.arange(lag_total) - lag_total // 2) * LSTEP
    bin_number = FIRST + np.arange(bin_count)
    phase_turns = lag_samples[:, None] * bin_number[None, :] % SEGLEN
    phase_angle = phase_turns.astype(np.float32) * np.float32(2.0 * math.pi / SEGLEN)
    return np.stack([np.cos(phase_angle), np.sin(phase_angle)], axis=1).astype(np.float32)


def mixed(index, offset):
    result = index
    bit = 1
    while bit <= offset:
        if offset & bit:
            result = result + bit - 2 * bit * ((index // bit) % 2)
        bit *= 2
    return result


def correlate_kernel(
    tiles, days, group, norm_factor, low_ref, high_ref, own_pair_ref, trig_ref, raw_ref, out_ref,
    own_ref, spread_ref, win_ref, gath_ref, pair_ref,
    rot_ref, part_ref, day_buf, send_buf, recv_buf, top_buf, down_src, down_buf,
    send_sem, recv_sem, far_send, far_recv, pair_send, pair_recv, up_send, up_recv, own_sem,
    day_send, day_recv, tile_send, tile_recv, top_send, top_recv, down_send, down_recv,
):
    here = lax.axis_index("tile")
    day = lax.axis_index("day")
    spot = here % group
    base = here - spot
    chunks = 2 * BLK_DEV
    has_below = base > 0
    has_above = base + group < tiles
    upper = REACH - BELOW

    last = group - 1
    is_top = base + group == tiles
    base_block = (base - BELOW) * BLK_DEV
    window_tiles, _, _, chans, _ = win_ref.shape
    lags = days
    rows_dev = out_ref.shape[1]

    barrier = pltpu.get_barrier_semaphore()
    for offset in range(1, days):
        pl.semaphore_signal(
            barrier, inc=1, device_id={"day": (day + offset) % days}, device_id_type=MESH
        )
    for offset in range(1, group):
        pl.semaphore_signal(
            barrier, inc=1, device_id={"tile": base + mixed(spot, offset)}, device_id_type=MESH
        )

    @pl.when(has_below)
    def _():
        pl.semaphore_signal(barrier, inc=1, device_id={"tile": here - group}, device_id_type=MESH)

    @pl.when(has_above)
    def _():
        pl.semaphore_signal(barrier, inc=1, device_id={"tile": here + group}, device_id_type=MESH)

    bins = raw_ref.shape[-1]
    row = lax.broadcasted_iota(jnp.int32, (bins, bins), 0)
    col = lax.broadcasted_iota(jnp.int32, (bins, bins), 1)
    spread_ref[...] = jnp.where(jnp.abs(row - col) <= HALF_WIN, 1.0, 0.0).astype(jnp.bfloat16)
    bin_index = lax.broadcasted_iota(jnp.int32, (1, bins), 1)
    counts = (
        jnp.minimum(bin_index + HALF_WIN, bins - 1) - jnp.maximum(bin_index - HALF_WIN, 0) + 1
    ).astype(jnp.float32)
    gath_ref[BELOW + spot, 0:rows_dev, 0:2] = own_pair_ref[...]

    @pl.when(base == 0)
    def _():
        gath_ref[0] = jnp.full(gath_ref.shape[1:], -1, jnp.int32)

    peers = days - 1 + group - 1 + has_below.astype(jnp.int32) + has_above.astype(jnp.int32)
    pl.semaphore_wait(barrier, peers)

    def whiten(there, block):
        real = raw_ref[there, 0, block].astype(jnp.float32)
        imag = raw_ref[there, 1, block].astype(jnp.float32)
        magnitude = jnp.sqrt(real * real + imag * imag)
        coarse = magnitude.astype(jnp.bfloat16)
        fine = (magnitude - coarse.astype(jnp.float32)).astype(jnp.bfloat16)
        spread = spread_ref[...]
        sums = jnp.dot(coarse, spread, preferred_element_type=jnp.float32) + jnp.dot(
            fine, spread, preferred_element_type=jnp.float32
        )
        amplitude = sums / counts + 1e-05
        keep = (bin_index >= low_ref[block]) & (bin_index < high_ref[block])
        gain = 1.0 / amplitude
        own_ref[there, 0, block] = jnp.where(keep, real * gain, 0.0).astype(jnp.bfloat16)
        own_ref[there, 1, block] = jnp.where(keep, imag * gain, 0.0).astype(jnp.bfloat16)

    def across(offset, chunk):
        block, part = divmod(chunk, 2)
        there = mixed(spot, offset)
        return pltpu.make_async_remote_copy(
            src_ref=own_ref.at[there, part, block],
            dst_ref=win_ref.at[BELOW + spot, part, block],
            send_sem=send_sem.at[offset - 1, chunk],
            recv_sem=recv_sem.at[offset - 1, chunk],
            device_id={"tile": base + there},
            device_id_type=MESH,
        )

    def pairs_across(offset):
        return pltpu.make_async_remote_copy(
            src_ref=gath_ref.at[BELOW + spot],
            dst_ref=gath_ref.at[BELOW + spot],
            send_sem=pair_send.at[offset - 1],
            recv_sem=pair_recv.at[offset - 1],
            device_id={"tile": base + mixed(spot, offset)},
            device_id_type=MESH,
        )

    def pairs_up():
        return pltpu.make_async_remote_copy(
            src_ref=gath_ref.at[group],
            dst_ref=gath_ref.at[0],
            send_sem=up_send,
            recv_sem=up_recv,
            device_id={"tile": here + group},
            device_id_type=MESH,
        )

    def far(source, slot, target, device, chunk):
        block, part = divmod(chunk, 2)
        index = 0 if target == 0 else target - BELOW - group + 1
        return pltpu.make_async_remote_copy(
            src_ref=source.at[slot, part, block],
            dst_ref=win_ref.at[target, part, block],
            send_sem=far_send.at[index, chunk],
            recv_sem=far_recv.at[index, chunk],
            device_id={"tile": device},
            device_id_type=MESH,
        )

    def relay(source, slot, where, chunk_list):
        for lower in range(upper):

            @pl.when(has_below & (where == lower))
            def _():
                for chunk in chunk_list:
                    far(source, slot, BELOW + group + lower, here - group, chunk).start()

        @pl.when(has_above & (where == group - 1))
        def _():
            for chunk in chunk_list:
                far(source, slot, 0, here + group, chunk).start()

    def send(offset, block):
        if offset:
            for part in range(2):
                across(offset, 2 * block + part).start()
        else:
            relay(own_ref, spot, spot, [2 * block, 2 * block + 1])

    turns = list(range(1, last)) + [0, last]
    items = [(offset, block) for block in range(BLK_DEV) for offset in turns]
    for index, (offset, block) in enumerate(items):
        whiten(mixed(spot, offset), block)
        if index:
            send(*items[index - 1])
        else:
            for peer in range(1, group):
                pairs_across(peer).start()
    send(*items[-1])
    stay = pltpu.make_async_copy(own_ref.at[spot], win_ref.at[BELOW + spot], own_sem)
    stay.start()

    for chunk in range(chunks):
        for offset in range(1, group):
            across(offset, chunk).wait_recv()
            there = mixed(spot, offset)
            relay(win_ref, BELOW + there, there, [chunk])

    def rotate(tile, carry):
        for block in range(BLK_DEV):
            real = win_ref[tile, 0, block].astype(jnp.float32)
            imag = win_ref[tile, 1, block].astype(jnp.float32)
            for lag in range(lags):
                cosine = trig_ref[lag, 0:1]
                sine = trig_ref[lag, 1:2]
                rows = slice(lag * chans, (lag + 1) * chans)
                rot_ref[tile * BLK_DEV + block, 0, rows] = (real * cosine + imag * sine).astype(
                    jnp.bfloat16
                )
                rot_ref[tile * BLK_DEV + block, 1, rows] = (imag * cosine - real * sine).astype(
                    jnp.bfloat16
                )
        return carry

    for chunk in range(chunks):
        for offset in range(1, group):
            across(offset, chunk).wait_send()
    stay.wait()
    for offset in range(1, group):
        pairs_across(offset).wait()

    @pl.when(has_above)
    def _():
        pairs_up().start()

    lax.fori_loop(BELOW, BELOW + group, rotate, 0)

    @pl.when(has_above)
    def _():
        pairs_up().wait_send()
        for chunk in range(chunks):
            far(own_ref, 0, 0, here + group, chunk).wait_send()
            for lower in range(upper):
                far(own_ref, 0, BELOW + group + lower, here, chunk).wait_recv()

    @pl.when(has_below)
    def _():
        pairs_up().wait_recv()
        for chunk in range(chunks):
            far(own_ref, 0, 0, here, chunk).wait_recv()
            for lower in range(upper):
                far(own_ref, 0, BELOW + group + lower, here - group, chunk).wait_send()

    gather_pairs = pltpu.make_async_copy(gath_ref, pair_ref, own_sem)
    gather_pairs.start()
    lax.fori_loop(0, BELOW, rotate, 0)
    lax.fori_loop(BELOW + group, window_tiles, rotate, 0)
    gather_pairs.wait()

    def products(set_index, slot):
        for row in range(rows_dev):
            first = pair_ref[set_index, row, 0]
            second = pair_ref[set_index, row, 1]
            left = jnp.clip(first - base_block, 0, window_tiles * BLK_DEV - 1)
            right = jnp.clip(second - base_block, 0, window_tiles * BLK_DEV - 1)
            total = jnp.zeros((chans, lags * chans), jnp.float32)
            for part in range(2):
                total = total + lax.dot_general(
                    win_ref[left // BLK_DEV, part, left % BLK_DEV],
                    rot_ref[right, part],
                    (((1,), (1,)), ((), ())),
                    preferred_element_type=jnp.float32,
                )
            total = jnp.where(first >= 0, total * norm_factor, 0.0)
            for lag in range(lags):
                part_ref[slot, lag, row] = total[:, lag * chans : (lag + 1) * chans]

    def day_copy(step, slot):
        target = (day + step) % days
        return pltpu.make_async_remote_copy(
            src_ref=part_ref.at[slot, target],
            dst_ref=day_buf.at[step - 1, slot],
            send_sem=day_send.at[step - 1, slot],
            recv_sem=day_recv.at[step - 1, slot],
            device_id={"day": target},
            device_id_type=MESH,
        )

    def day_total(slot):
        total = part_ref[slot, day]
        for step in range(1, days):
            day_copy(step, slot).wait_recv()
            total = total + day_buf[step - 1, slot]
        return total

    def tile_copy(target, source):
        return pltpu.make_async_remote_copy(
            src_ref=send_buf.at[target],
            dst_ref=recv_buf.at[source],
            send_sem=tile_send.at[target],
            recv_sem=tile_recv.at[source],
            device_id={"tile": base + target},
            device_id_type=MESH,
        )

    def top_copy(device, slot):
        return pltpu.make_async_remote_copy(
            src_ref=send_buf.at[group],
            dst_ref=top_buf.at[slot],
            send_sem=top_send,
            recv_sem=top_recv.at[slot],
            device_id={"tile": device},
            device_id_type=MESH,
        )

    def down_copy(row, device):
        return pltpu.make_async_remote_copy(
            src_ref=down_src.at[row],
            dst_ref=down_buf.at[row],
            send_sem=down_send.at[row],
            recv_sem=down_recv.at[row],
            device_id={"tile": device},
            device_id_type=MESH,
        )

    def destination(step):
        return (spot + step) % last if step else jnp.int32(last)

    def push(step):
        target = destination(step)
        total = day_total(target)

        @pl.when(target == spot)
        def _():
            out_ref[0] = total

        @pl.when(target != spot)
        def _():
            send_buf[target] = total.astype(jnp.bfloat16)
            tile_copy(target, spot).start()

    for turn in range(group):
        target = destination(turn)
        products((target + BELOW) % group, target)
        for step in range(1, days):
            day_copy(step, target).start()
        if turn:
            push(turn - 1)

    @pl.when(is_top)
    def _():
        products(group, group)
        for step in range(1, days):
            day_copy(step, group).start()

    push(last)

    @pl.when(is_top)
    def _():
        total = day_total(group)

        @pl.when(spot < last)
        def _():
            send_buf[group] = total.astype(jnp.bfloat16)
            top_copy(base + last, spot).start()

        @pl.when(spot == last)
        def _():
            part_ref[group, day] = total

    for offset in range(last, 0, -1):
        tile_copy(spot, mixed(spot, offset)).wait_recv()
    sends_down = has_below & (spot == last)
    takes_down = has_above & (spot == last)
    for row in range(rows_dev):
        total = out_ref[0, row]
        for offset in range(last, 0, -1):
            total = total + recv_buf[mixed(spot, offset), row].astype(jnp.float32)
        out_ref[0, row] = total

        @pl.when(sends_down)
        def _():
            down_src[row] = total.astype(jnp.bfloat16)
            down_copy(row, here - group).start()

    @pl.when(takes_down)
    def _():
        for row in range(rows_dev):
            down_copy(row, here).wait_recv()
            out_ref[0, row] = down_buf[row].astype(jnp.float32)

    @pl.when(is_top & (spot == last))
    def _():
        total = part_ref[group, day]
        for slot in range(last):
            top_copy(here, slot).wait_recv()
            total = total + top_buf[slot].astype(jnp.float32)
        out_ref[0] = total

    @pl.when(is_top & (spot < last))
    def _():
        top_copy(base + last, spot).wait_send()

    @pl.when(sends_down)
    def _():
        for row in range(rows_dev):
            down_copy(row, here - group).wait_send()

    for offset in range(last, 0, -1):
        tile_copy(mixed(spot, offset), spot).wait_send()
    for offset in range(last, -1, -1):
        for step in range(1, days):
            day_copy(step, offset).wait_send()

    @pl.when(is_top)
    def _():
        for step in range(1, days):
            day_copy(step, group).wait_send()


def per_device(tiles, days, spectra, band_low, band_high, pair_list):
    own = spectra[0]
    channels, parts, segments, bins = own.shape
    group = segments
    chans = channels // BLK_DEV
    rows_dev = pair_list.shape[0]
    lags = days
    norm_factor = 1.0 / math.sqrt(segments * bins * days)
    slice_shape = (parts, BLK_DEV, chans, bins)
    raw = jnp.transpose(own.reshape(BLK_DEV, chans, parts, segments, bins), (3, 2, 0, 1, 4))

    chunks = 2 * BLK_DEV
    block_shape = (rows_dev, chans, chans)
    gathered_shape = (BELOW + group, 8, 128)
    return pl.pallas_call(
        functools.partial(correlate_kernel, tiles, days, group, norm_factor),
        out_shape=jax.ShapeDtypeStruct((1,) + block_shape, jnp.float32),
        in_specs=[SMEM, SMEM, VMEM, VMEM, VMEM],
        out_specs=VMEM,
        scratch_shapes=[
            pltpu.VMEM((segments,) + slice_shape, jnp.bfloat16),
            pltpu.VMEM((bins, bins), jnp.bfloat16),
            pltpu.VMEM((group + REACH,) + slice_shape, jnp.bfloat16),
            pltpu.VMEM(gathered_shape, jnp.int32),
            pltpu.SMEM(gathered_shape, jnp.int32),
            pltpu.VMEM(((group + REACH) * BLK_DEV, parts, lags * chans, bins), jnp.bfloat16),
            pltpu.VMEM((group + 1, lags) + block_shape, jnp.float32),
            pltpu.VMEM((days - 1, group + 1) + block_shape, jnp.float32),
            pltpu.VMEM((group + 1,) + block_shape, jnp.bfloat16),
            pltpu.VMEM((group,) + block_shape, jnp.bfloat16),
            pltpu.VMEM((group - 1,) + block_shape, jnp.bfloat16),
            pltpu.VMEM(block_shape, jnp.bfloat16),
            pltpu.VMEM(block_shape, jnp.bfloat16),
            pltpu.SemaphoreType.DMA((group - 1, chunks)),
            pltpu.SemaphoreType.DMA((group - 1, chunks)),
            pltpu.SemaphoreType.DMA((REACH, chunks)),
            pltpu.SemaphoreType.DMA((REACH, chunks)),
            pltpu.SemaphoreType.DMA((group - 1,)),
            pltpu.SemaphoreType.DMA((group - 1,)),
            pltpu.SemaphoreType.DMA,
            pltpu.SemaphoreType.DMA,
            pltpu.SemaphoreType.DMA,
            pltpu.SemaphoreType.DMA((days - 1, group + 1)),
            pltpu.SemaphoreType.DMA((days - 1, group + 1)),
            pltpu.SemaphoreType.DMA((group,)),
            pltpu.SemaphoreType.DMA((group,)),
            pltpu.SemaphoreType.DMA,
            pltpu.SemaphoreType.DMA((group - 1,)),
            pltpu.SemaphoreType.DMA((rows_dev,)),
            pltpu.SemaphoreType.DMA((rows_dev,)),
        ],
        compiler_params=pltpu.CompilerParams(
            collective_id=0, has_side_effects=True, vmem_limit_bytes=63 * 1024 * 1024
        ),
    )(band_low, band_high, pair_list, jnp.asarray(phase_tables(lags, bins)), raw)


def solution(mesh):
    placed = (P("day", "tile", None, None, None), P("tile"), P("tile"), P("tile", None))
    return jax.shard_map(
        functools.partial(per_device, mesh.shape["tile"], mesh.shape["day"]),
        mesh=mesh,
        in_specs=placed,
        out_specs=P("day", "tile", None, None),
        check_vma=False,
    )
```

```python
import functools
import math

import jax
import jax.numpy as jnp
import numpy as np
from jax import lax
from jax.experimental import pallas as pl
from jax.experimental.pallas import tpu as pltpu
from jax.sharding import PartitionSpec as P

BLK_DEV = 2
SEGLEN = 15000
FIRST = 90
HALF_WIN = 64
LSTEP = 25
REACH = 3
BELOW = 1
MESH = pl.DeviceIdType.MESH
VMEM = pl.BlockSpec(memory_space=pltpu.VMEM)
SMEM = pl.BlockSpec(memory_space=pltpu.SMEM)


def phase_tables(lag_total, bin_count):
    lag_samples = (np.arange(lag_total) - lag_total // 2) * LSTEP
    bin_number = FIRST + np.arange(bin_count)
    phase_turns = lag_samples[:, None] * bin_number[None, :] % SEGLEN
    phase_angle = phase_turns.astype(np.float32) * np.float32(2.0 * math.pi / SEGLEN)
    return np.stack([np.cos(phase_angle), np.sin(phase_angle)], axis=1).astype(np.float32)


def mixed(index, offset):
    result = index
    bit = 1
    while bit <= offset:
        if offset & bit:
            result = result + bit - 2 * bit * ((index // bit) % 2)
        bit *= 2
    return result


def correlate_kernel(
    tiles, days, group, norm_factor, low_ref, high_ref, own_pair_ref, trig_ref, raw_ref, out_ref,
    own_ref, spread_ref, win_ref, gath_ref, pair_ref,
    rot_ref, part_ref, day_buf, send_buf, recv_buf, top_buf, down_src, down_buf,
    send_sem, recv_sem, far_send, far_recv, pair_send, pair_recv, up_send, up_recv, own_sem,
    day_send, day_recv, tile_send, tile_recv, top_send, top_recv, down_send, down_recv,
):
    here = lax.axis_index("tile")
    day = lax.axis_index("day")
    spot = here % group
    base = here - spot
    chunks = 2 * BLK_DEV
    has_below = base > 0
    has_above = base + group < tiles
    upper = REACH - BELOW

    last = group - 1
    is_top = base + group == tiles
    base_block = (base - BELOW) * BLK_DEV
    window_tiles, _, _, chans, _ = win_ref.shape
    lags = days
    rows_dev = out_ref.shape[1]

    barrier = pltpu.get_barrier_semaphore()
    for offset in range(1, days):
        pl.semaphore_signal(
            barrier, inc=1, device_id={"day": (day + offset) % days}, device_id_type=MESH
        )
    for offset in range(1, group):
        pl.semaphore_signal(
            barrier, inc=1, device_id={"tile": base + mixed(spot, offset)}, device_id_type=MESH
        )

    @pl.when(has_below)
    def _():
        pl.semaphore_signal(barrier, inc=1, device_id={"tile": here - group}, device_id_type=MESH)

    @pl.when(has_above)
    def _():
        pl.semaphore_signal(barrier, inc=1, device_id={"tile": here + group}, device_id_type=MESH)

    bins = raw_ref.shape[-1]
    row = lax.broadcasted_iota(jnp.int32, (bins, bins), 0)
    col = lax.broadcasted_iota(jnp.int32, (bins, bins), 1)
    spread_ref[...] = jnp.where(jnp.abs(row - col) <= HALF_WIN, 1.0, 0.0).astype(jnp.bfloat16)
    bin_index = lax.broadcasted_iota(jnp.int32, (1, bins), 1)
    counts = (
        jnp.minimum(bin_index + HALF_WIN, bins - 1) - jnp.maximum(bin_index - HALF_WIN, 0) + 1
    ).astype(jnp.float32)
    gath_ref[BELOW + spot, 0:2, 0:rows_dev] = own_pair_ref[...]

    @pl.when(base == 0)
    def _():
        gath_ref[0] = jnp.full(gath_ref.shape[1:], -1, jnp.int32)

    peers = days - 1 + group - 1 + has_below.astype(jnp.int32) + has_above.astype(jnp.int32)
    pl.semaphore_wait(barrier, peers)

    def whiten(there, block):
        real = raw_ref[there, 0, block].astype(jnp.float32)
        imag = raw_ref[there, 1, block].astype(jnp.float32)
        magnitude = jnp.sqrt(real * real + imag * imag)
        coarse = magnitude.astype(jnp.bfloat16)
        fine = (magnitude - coarse.astype(jnp.float32)).astype(jnp.bfloat16)
        spread = spread_ref[...]
        sums = jnp.dot(coarse, spread, preferred_element_type=jnp.float32) + jnp.dot(
            fine, spread, preferred_element_type=jnp.float32
        )
        amplitude = sums / counts + 1e-05
        keep = (bin_index >= low_ref[block]) & (bin_index < high_ref[block])
        gain = 1.0 / amplitude
        own_ref[there, 0, block] = jnp.where(keep, real * gain, 0.0).astype(jnp.bfloat16)
        own_ref[there, 1, block] = jnp.where(keep, imag * gain, 0.0).astype(jnp.bfloat16)

    def across(offset, chunk):
        block, part = divmod(chunk, 2)
        there = mixed(spot, offset)
        return pltpu.make_async_remote_copy(
            src_ref=own_ref.at[there, part, block],
            dst_ref=win_ref.at[BELOW + spot, part, block],
            send_sem=send_sem.at[offset - 1, chunk],
            recv_sem=recv_sem.at[offset - 1, chunk],
            device_id={"tile": base + there},
            device_id_type=MESH,
        )

    def pairs_across(offset):
        return pltpu.make_async_remote_copy(
            src_ref=gath_ref.at[BELOW + spot],
            dst_ref=gath_ref.at[BELOW + spot],
            send_sem=pair_send.at[offset - 1],
            recv_sem=pair_recv.at[offset - 1],
            device_id={"tile": base + mixed(spot, offset)},
            device_id_type=MESH,
        )

    def pairs_up():
        return pltpu.make_async_remote_copy(
            src_ref=gath_ref.at[group],
            dst_ref=gath_ref.at[0],
            send_sem=up_send,
            recv_sem=up_recv,
            device_id={"tile": here + group},
            device_id_type=MESH,
        )

    def far(source, slot, target, device, chunk):
        block, part = divmod(chunk, 2)
        index = 0 if target == 0 else target - BELOW - group + 1
        return pltpu.make_async_remote_copy(
            src_ref=source.at[slot, part, block],
            dst_ref=win_ref.at[target, part, block],
            send_sem=far_send.at[index, chunk],
            recv_sem=far_recv.at[index, chunk],
            device_id={"tile": device},
            device_id_type=MESH,
        )

    def relay(source, slot, where, chunk_list):
        for lower in range(upper):

            @pl.when(has_below & (where == lower))
            def _():
                for chunk in chunk_list:
                    far(source, slot, BELOW + group + lower, here - group, chunk).start()

        @pl.when(has_above & (where == group - 1))
        def _():
            for chunk in chunk_list:
                far(source, slot, 0, here + group, chunk).start()

    def send(offset, block):
        if offset:
            for part in range(2):
                across(offset, 2 * block + part).start()
        else:
            relay(own_ref, spot, spot, [2 * block, 2 * block + 1])

    turns = list(range(1, last)) + [0, last]
    items = [(offset, block) for block in range(BLK_DEV) for offset in turns]
    for index, (offset, block) in enumerate(items):
        whiten(mixed(spot, offset), block)
        if index:
            send(*items[index - 1])
        else:
            for peer in range(1, group):
                pairs_across(peer).start()
    send(*items[-1])
    stay = pltpu.make_async_copy(own_ref.at[spot], win_ref.at[BELOW + spot], own_sem)
    stay.start()

    for chunk in range(chunks):
        for offset in range(1, group):
            across(offset, chunk).wait_recv()
            there = mixed(spot, offset)
            relay(win_ref, BELOW + there, there, [chunk])

    def rotate(tile, carry):
        for block in range(BLK_DEV):
            real = win_ref[tile, 0, block].astype(jnp.float32)
            imag = win_ref[tile, 1, block].astype(jnp.float32)
            for lag in range(lags):
                cosine = trig_ref[lag, 0:1]
                sine = trig_ref[lag, 1:2]
                rows = slice(lag * chans, (lag + 1) * chans)
                rot_ref[tile * BLK_DEV + block, 0, rows] = (real * cosine + imag * sine).astype(
                    jnp.bfloat16
                )
                rot_ref[tile * BLK_DEV + block, 1, rows] = (imag * cosine - real * sine).astype(
                    jnp.bfloat16
                )
        return carry

    for chunk in range(chunks):
        for offset in range(1, group):
            across(offset, chunk).wait_send()
    stay.wait()
    for offset in range(1, group):
        pairs_across(offset).wait()

    @pl.when(has_above)
    def _():
        pairs_up().start()

    lax.fori_loop(BELOW, BELOW + group, rotate, 0)

    @pl.when(has_above)
    def _():
        pairs_up().wait_send()
        for chunk in range(chunks):
            far(own_ref, 0, 0, here + group, chunk).wait_send()
            for lower in range(upper):
                far(own_ref, 0, BELOW + group + lower, here, chunk).wait_recv()

    @pl.when(has_below)
    def _():
        pairs_up().wait_recv()
        for chunk in range(chunks):
            far(own_ref, 0, 0, here, chunk).wait_recv()
            for lower in range(upper):
                far(own_ref, 0, BELOW + group + lower, here - group, chunk).wait_send()

    gather_pairs = pltpu.make_async_copy(gath_ref, pair_ref, own_sem)
    gather_pairs.start()
    lax.fori_loop(0, BELOW, rotate, 0)
    lax.fori_loop(BELOW + group, window_tiles, rotate, 0)
    gather_pairs.wait()

    def products(set_index, slot):
        for row in range(rows_dev):
            first = pair_ref[set_index, 0, row]
            second = pair_ref[set_index, 1, row]
            left = jnp.clip(first - base_block, 0, window_tiles * BLK_DEV - 1)
            right = jnp.clip(second - base_block, 0, window_tiles * BLK_DEV - 1)
            total = jnp.zeros((chans, lags * chans), jnp.float32)
            for part in range(2):
                total = total + lax.dot_general(
                    win_ref[left // BLK_DEV, part, left % BLK_DEV],
                    rot_ref[right, part],
                    (((1,), (1,)), ((), ())),
                    preferred_element_type=jnp.float32,
                )
            total = jnp.where(first >= 0, total * norm_factor, 0.0)
            for lag in range(lags):
                part_ref[slot, lag, row] = total[:, lag * chans : (lag + 1) * chans]

    def day_copy(step, slot):
        target = (day + step) % days
        return pltpu.make_async_remote_copy(
            src_ref=part_ref.at[slot, target],
            dst_ref=day_buf.at[step - 1, slot],
            send_sem=day_send.at[step - 1, slot],
            recv_sem=day_recv.at[step - 1, slot],
            device_id={"day": target},
            device_id_type=MESH,
        )

    def day_total(slot):
        total = part_ref[slot, day]
        for step in range(1, days):
            day_copy(step, slot).wait_recv()
            total = total + day_buf[step - 1, slot]
        return total

    def tile_copy(target, source):
        return pltpu.make_async_remote_copy(
            src_ref=send_buf.at[target],
            dst_ref=recv_buf.at[source],
            send_sem=tile_send.at[target],
            recv_sem=tile_recv.at[source],
            device_id={"tile": base + target},
            device_id_type=MESH,
        )

    def top_copy(device, slot):
        return pltpu.make_async_remote_copy(
            src_ref=send_buf.at[group],
            dst_ref=top_buf.at[slot],
            send_sem=top_send,
            recv_sem=top_recv.at[slot],
            device_id={"tile": device},
            device_id_type=MESH,
        )

    def down_copy(row, device):
        return pltpu.make_async_remote_copy(
            src_ref=down_src.at[row],
            dst_ref=down_buf.at[row],
            send_sem=down_send.at[row],
            recv_sem=down_recv.at[row],
            device_id={"tile": device},
            device_id_type=MESH,
        )

    def destination(step):
        is_last = spot // last
        return is_last * step + (1 - is_last) * ((spot + step) % last if step else last)

    def push(step):
        target = destination(step)
        total = day_total(target)

        @pl.when(target == spot)
        def _():
            out_ref[0] = total

        @pl.when(target != spot)
        def _():
            send_buf[target] = total.astype(jnp.bfloat16)
            tile_copy(target, spot).start()

    for turn in range(group):
        target = destination(turn)
        products((target + BELOW) % group, target)
        for step in range(1, days):
            day_copy(step, target).start()
        if turn:
            push(turn - 1)

    @pl.when(is_top)
    def _():
        products(group, group)
        for step in range(1, days):
            day_copy(step, group).start()

    push(last)

    @pl.when(is_top)
    def _():
        total = day_total(group)

        @pl.when(spot < last)
        def _():
            send_buf[group] = total.astype(jnp.bfloat16)
            top_copy(base + last, spot).start()

        @pl.when(spot == last)
        def _():
            part_ref[group, day] = total

    for offset in range(last, 0, -1):
        tile_copy(spot, mixed(spot, offset)).wait_recv()
    sends_down = has_below & (spot == last)
    takes_down = has_above & (spot == last)
    for row in range(rows_dev):
        total = out_ref[0, row]
        for offset in range(last, 0, -1):
            total = total + recv_buf[mixed(spot, offset), row].astype(jnp.float32)
        out_ref[0, row] = total

        @pl.when(sends_down)
        def _():
            down_src[row] = total.astype(jnp.bfloat16)
            down_copy(row, here - group).start()

    @pl.when(takes_down)
    def _():
        for row in range(rows_dev):
            down_copy(row, here).wait_recv()
            out_ref[0, row] = down_buf[row].astype(jnp.float32)

    @pl.when(is_top & (spot == last))
    def _():
        total = part_ref[group, day]
        for slot in range(last):
            top_copy(here, slot).wait_recv()
            total = total + top_buf[slot].astype(jnp.float32)
        out_ref[0] = total

    @pl.when(is_top & (spot < last))
    def _():
        top_copy(base + last, spot).wait_send()

    @pl.when(sends_down)
    def _():
        for row in range(rows_dev):
            down_copy(row, here - group).wait_send()

    for offset in range(last, 0, -1):
        tile_copy(mixed(spot, offset), spot).wait_send()
    for offset in range(last, -1, -1):
        for step in range(1, days):
            day_copy(step, offset).wait_send()

    @pl.when(is_top)
    def _():
        for step in range(1, days):
            day_copy(step, group).wait_send()


def per_device(tiles, days, spectra, band_low, band_high, pair_list):
    own = spectra[0]
    channels, parts, segments, bins = own.shape
    group = segments
    chans = channels // BLK_DEV
    rows_dev = pair_list.shape[0]
    lags = days
    norm_factor = 1.0 / math.sqrt(segments * bins * days)
    slice_shape = (parts, BLK_DEV, chans, bins)
    raw = jnp.transpose(own.reshape(BLK_DEV, chans, parts, segments, bins), (3, 2, 0, 1, 4))

    chunks = 2 * BLK_DEV
    block_shape = (rows_dev, chans, chans)
    gathered_shape = (BELOW + group, 8, 128)
    return pl.pallas_call(
        functools.partial(correlate_kernel, tiles, days, group, norm_factor),
        out_shape=jax.ShapeDtypeStruct((1,) + block_shape, jnp.float32),
        in_specs=[SMEM, SMEM, VMEM, VMEM, VMEM],
        out_specs=VMEM,
        scratch_shapes=[
            pltpu.VMEM((segments,) + slice_shape, jnp.bfloat16),
            pltpu.VMEM((bins, bins), jnp.bfloat16),
            pltpu.VMEM((group + REACH,) + slice_shape, jnp.bfloat16),
            pltpu.VMEM(gathered_shape, jnp.int32),
            pltpu.SMEM(gathered_shape, jnp.int32),
            pltpu.VMEM(((group + REACH) * BLK_DEV, parts, lags * chans, bins), jnp.bfloat16),
            pltpu.VMEM((group + 1, lags) + block_shape, jnp.float32),
            pltpu.VMEM((days - 1, group + 1) + block_shape, jnp.float32),
            pltpu.VMEM((group + 1,) + block_shape, jnp.bfloat16),
            pltpu.VMEM((group,) + block_shape, jnp.bfloat16),
            pltpu.VMEM((group - 1,) + block_shape, jnp.bfloat16),
            pltpu.VMEM(block_shape, jnp.bfloat16),
            pltpu.VMEM(block_shape, jnp.bfloat16),
            pltpu.SemaphoreType.DMA((group - 1, chunks)),
            pltpu.SemaphoreType.DMA((group - 1, chunks)),
            pltpu.SemaphoreType.DMA((REACH, chunks)),
            pltpu.SemaphoreType.DMA((REACH, chunks)),
            pltpu.SemaphoreType.DMA((group - 1,)),
            pltpu.SemaphoreType.DMA((group - 1,)),
            pltpu.SemaphoreType.DMA,
            pltpu.SemaphoreType.DMA,
            pltpu.SemaphoreType.DMA,
            pltpu.SemaphoreType.DMA((days - 1, group + 1)),
            pltpu.SemaphoreType.DMA((days - 1, group + 1)),
            pltpu.SemaphoreType.DMA((group,)),
            pltpu.SemaphoreType.DMA((group,)),
            pltpu.SemaphoreType.DMA,
            pltpu.SemaphoreType.DMA((group - 1,)),
            pltpu.SemaphoreType.DMA((rows_dev,)),
            pltpu.SemaphoreType.DMA((rows_dev,)),
        ],
        compiler_params=pltpu.CompilerParams(
            collective_id=0, has_side_effects=True, vmem_limit_bytes=63 * 1024 * 1024
        ),
    )(band_low, band_high, pair_list.T, jnp.asarray(phase_tables(lags, bins)), raw)


def solution(mesh):
    placed = (P("day", "tile", None, None, None), P("tile"), P("tile"), P("tile", None))
    return jax.shard_map(
        functools.partial(per_device, mesh.shape["tile"], mesh.shape["day"]),
        mesh=mesh,
        in_specs=placed,
        out_specs=P("day", "tile", None, None),
        check_vma=False,
    )
```

```python
import functools
import math

import jax
import jax.numpy as jnp
import numpy as np
from jax import lax
from jax.experimental import pallas as pl
from jax.experimental.pallas import tpu as pltpu
from jax.sharding import PartitionSpec as P

BLK_DEV = 2
SEGLEN = 15000
FIRST = 90
HALF_WIN = 64
LSTEP = 25
REACH = 3
BELOW = 1
MESH = pl.DeviceIdType.MESH
VMEM = pl.BlockSpec(memory_space=pltpu.VMEM)
SMEM = pl.BlockSpec(memory_space=pltpu.SMEM)


def phase_tables(lag_total, bin_count):
    lag_samples = (np.arange(lag_total) - lag_total // 2) * LSTEP
    bin_number = FIRST + np.arange(bin_count)
    phase_turns = lag_samples[:, None] * bin_number[None, :] % SEGLEN
    phase_angle = phase_turns.astype(np.float32) * np.float32(2.0 * math.pi / SEGLEN)
    return np.stack([np.cos(phase_angle), np.sin(phase_angle)], axis=1).astype(np.float32)


def mixed(index, offset):
    result = index
    bit = 1
    while bit <= offset:
        if offset & bit:
            result = result + bit - 2 * bit * ((index // bit) % 2)
        bit *= 2
    return result


def correlate_kernel(
    tiles, days, group, norm_factor, low_ref, high_ref, own_pair_ref, trig_ref, raw_hbm, out_ref,
    raw_ref, raw_sem, own_ref, spread_ref, win_ref, gath_ref, pair_ref,
    rot_ref, part_ref, day_buf, send_buf, recv_buf, top_buf, down_src, down_buf,
    send_sem, recv_sem, far_send, far_recv, pair_send, pair_recv, up_send, up_recv, own_sem,
    day_send, day_recv, tile_send, tile_recv, top_send, top_recv, down_send, down_recv,
):
    here = lax.axis_index("tile")
    day = lax.axis_index("day")
    spot = here % group
    base = here - spot
    chunks = 2 * BLK_DEV
    has_below = base > 0
    has_above = base + group < tiles
    upper = REACH - BELOW

    last = group - 1
    turns = list(range(1, last)) + [0, last]
    items = [(offset, block) for block in range(BLK_DEV) for offset in turns]

    def fetch(offset, block):
        there = mixed(spot, offset)
        return pltpu.make_async_copy(
            raw_hbm.at[there, :, block], raw_ref.at[there, :, block], raw_sem.at[offset, block]
        )

    for item in items:
        fetch(*item).start()
    is_top = base + group == tiles
    base_block = (base - BELOW) * BLK_DEV
    window_tiles, _, _, chans, _ = win_ref.shape
    lags = days
    rows_dev = out_ref.shape[1]

    barrier = pltpu.get_barrier_semaphore()
    for offset in range(1, days):
        pl.semaphore_signal(
            barrier, inc=1, device_id={"day": (day + offset) % days}, device_id_type=MESH
        )
    for offset in range(1, group):
        pl.semaphore_signal(
            barrier, inc=1, device_id={"tile": base + mixed(spot, offset)}, device_id_type=MESH
        )

    @pl.when(has_below)
    def _():
        pl.semaphore_signal(barrier, inc=1, device_id={"tile": here - group}, device_id_type=MESH)

    @pl.when(has_above)
    def _():
        pl.semaphore_signal(barrier, inc=1, device_id={"tile": here + group}, device_id_type=MESH)

    bins = raw_ref.shape[-1]
    row = lax.broadcasted_iota(jnp.int32, (bins, bins), 0)
    col = lax.broadcasted_iota(jnp.int32, (bins, bins), 1)
    spread_ref[...] = jnp.where(jnp.abs(row - col) <= HALF_WIN, 1.0, 0.0).astype(jnp.bfloat16)
    bin_index = lax.broadcasted_iota(jnp.int32, (1, bins), 1)
    counts = (
        jnp.minimum(bin_index + HALF_WIN, bins - 1) - jnp.maximum(bin_index - HALF_WIN, 0) + 1
    ).astype(jnp.float32)
    gath_ref[BELOW + spot, 0:2, 0:rows_dev] = own_pair_ref[...]

    @pl.when(base == 0)
    def _():
        gath_ref[0] = jnp.full(gath_ref.shape[1:], -1, jnp.int32)

    peers = days - 1 + group - 1 + has_below.astype(jnp.int32) + has_above.astype(jnp.int32)
    pl.semaphore_wait(barrier, peers)

    def whiten(there, block):
        real = raw_ref[there, 0, block].astype(jnp.float32)
        imag = raw_ref[there, 1, block].astype(jnp.float32)
        magnitude = jnp.sqrt(real * real + imag * imag)
        coarse = magnitude.astype(jnp.bfloat16)
        fine = (magnitude - coarse.astype(jnp.float32)).astype(jnp.bfloat16)
        spread = spread_ref[...]
        sums = jnp.dot(coarse, spread, preferred_element_type=jnp.float32) + jnp.dot(
            fine, spread, preferred_element_type=jnp.float32
        )
        amplitude = sums / counts + 1e-05
        keep = (bin_index >= low_ref[block]) & (bin_index < high_ref[block])
        gain = 1.0 / amplitude
        own_ref[there, 0, block] = jnp.where(keep, real * gain, 0.0).astype(jnp.bfloat16)
        own_ref[there, 1, block] = jnp.where(keep, imag * gain, 0.0).astype(jnp.bfloat16)

    def across(offset, chunk):
        block, part = divmod(chunk, 2)
        there = mixed(spot, offset)
        return pltpu.make_async_remote_copy(
            src_ref=own_ref.at[there, part, block],
            dst_ref=win_ref.at[BELOW + spot, part, block],
            send_sem=send_sem.at[offset - 1, chunk],
            recv_sem=recv_sem.at[offset - 1, chunk],
            device_id={"tile": base + there},
            device_id_type=MESH,
        )

    def pairs_across(offset):
        return pltpu.make_async_remote_copy(
            src_ref=gath_ref.at[BELOW + spot],
            dst_ref=gath_ref.at[BELOW + spot],
            send_sem=pair_send.at[offset - 1],
            recv_sem=pair_recv.at[offset - 1],
            device_id={"tile": base + mixed(spot, offset)},
            device_id_type=MESH,
        )

    def pairs_up():
        return pltpu.make_async_remote_copy(
            src_ref=gath_ref.at[group],
            dst_ref=gath_ref.at[0],
            send_sem=up_send,
            recv_sem=up_recv,
            device_id={"tile": here + group},
            device_id_type=MESH,
        )

    def far(source, slot, target, device, chunk):
        block, part = divmod(chunk, 2)
        index = 0 if target == 0 else target - BELOW - group + 1
        return pltpu.make_async_remote_copy(
            src_ref=source.at[slot, part, block],
            dst_ref=win_ref.at[target, part, block],
            send_sem=far_send.at[index, chunk],
            recv_sem=far_recv.at[index, chunk],
            device_id={"tile": device},
            device_id_type=MESH,
        )

    def relay(source, slot, where, chunk_list):
        for lower in range(upper):

            @pl.when(has_below & (where == lower))
            def _():
                for chunk in chunk_list:
                    far(source, slot, BELOW + group + lower, here - group, chunk).start()

        @pl.when(has_above & (where == group - 1))
        def _():
            for chunk in chunk_list:
                far(source, slot, 0, here + group, chunk).start()

    def send(offset, block):
        if offset:
            for part in range(2):
                across(offset, 2 * block + part).start()
        else:
            relay(own_ref, spot, spot, [2 * block, 2 * block + 1])

    for index, (offset, block) in enumerate(items):
        fetch(offset, block).wait()
        whiten(mixed(spot, offset), block)
        if index:
            send(*items[index - 1])
        else:
            for peer in range(1, group):
                pairs_across(peer).start()
    send(*items[-1])
    stay = pltpu.make_async_copy(own_ref.at[spot], win_ref.at[BELOW + spot], own_sem)
    stay.start()

    for chunk in range(chunks):
        for offset in range(1, group):
            across(offset, chunk).wait_recv()
            there = mixed(spot, offset)
            relay(win_ref, BELOW + there, there, [chunk])

    def rotate(tile, carry):
        for block in range(BLK_DEV):
            real = win_ref[tile, 0, block].astype(jnp.float32)
            imag = win_ref[tile, 1, block].astype(jnp.float32)
            for lag in range(lags):
                cosine = trig_ref[lag, 0:1]
                sine = trig_ref[lag, 1:2]
                rows = slice(lag * chans, (lag + 1) * chans)
                rot_ref[tile * BLK_DEV + block, 0, rows] = (real * cosine + imag * sine).astype(
                    jnp.bfloat16
                )
                rot_ref[tile * BLK_DEV + block, 1, rows] = (imag * cosine - real * sine).astype(
                    jnp.bfloat16
                )
        return carry

    for chunk in range(chunks):
        for offset in range(1, group):
            across(offset, chunk).wait_send()
    stay.wait()
    for offset in range(1, group):
        pairs_across(offset).wait()

    @pl.when(has_above)
    def _():
        pairs_up().start()

    lax.fori_loop(BELOW, BELOW + group, rotate, 0)

    @pl.when(has_above)
    def _():
        pairs_up().wait_send()
        for chunk in range(chunks):
            far(own_ref, 0, 0, here + group, chunk).wait_send()
            for lower in range(upper):
                far(own_ref, 0, BELOW + group + lower, here, chunk).wait_recv()

    @pl.when(has_below)
    def _():
        pairs_up().wait_recv()
        for chunk in range(chunks):
            far(own_ref, 0, 0, here, chunk).wait_recv()
            for lower in range(upper):
                far(own_ref, 0, BELOW + group + lower, here - group, chunk).wait_send()

    gather_pairs = pltpu.make_async_copy(gath_ref, pair_ref, own_sem)
    gather_pairs.start()
    lax.fori_loop(0, BELOW, rotate, 0)
    lax.fori_loop(BELOW + group, window_tiles, rotate, 0)
    gather_pairs.wait()

    def products(set_index, slot):
        for row in range(rows_dev):
            first = pair_ref[set_index, 0, row]
            second = pair_ref[set_index, 1, row]
            left = jnp.clip(first - base_block, 0, window_tiles * BLK_DEV - 1)
            right = jnp.clip(second - base_block, 0, window_tiles * BLK_DEV - 1)
            total = jnp.zeros((chans, lags * chans), jnp.float32)
            for part in range(2):
                total = total + lax.dot_general(
                    win_ref[left // BLK_DEV, part, left % BLK_DEV],
                    rot_ref[right, part],
                    (((1,), (1,)), ((), ())),
                    preferred_element_type=jnp.float32,
                )
            total = jnp.where(first >= 0, total * norm_factor, 0.0)
            for lag in range(lags):
                part_ref[slot, lag, row] = total[:, lag * chans : (lag + 1) * chans]

    def day_copy(step, slot):
        target = (day + step) % days
        return pltpu.make_async_remote_copy(
            src_ref=part_ref.at[slot, target],
            dst_ref=day_buf.at[step - 1, slot],
            send_sem=day_send.at[step - 1, slot],
            recv_sem=day_recv.at[step - 1, slot],
            device_id={"day": target},
            device_id_type=MESH,
        )

    def day_total(slot):
        total = part_ref[slot, day]
        for step in range(1, days):
            day_copy(step, slot).wait_recv()
            total = total + day_buf[step - 1, slot]
        return total

    def tile_copy(target, source):
        return pltpu.make_async_remote_copy(
            src_ref=send_buf.at[target],
            dst_ref=recv_buf.at[source],
            send_sem=tile_send.at[target],
            recv_sem=tile_recv.at[source],
            device_id={"tile": base + target},
            device_id_type=MESH,
        )

    def top_copy(device, slot):
        return pltpu.make_async_remote_copy(
            src_ref=send_buf.at[group],
            dst_ref=top_buf.at[slot],
            send_sem=top_send,
            recv_sem=top_recv.at[slot],
            device_id={"tile": device},
            device_id_type=MESH,
        )

    def down_copy(row, device):
        return pltpu.make_async_remote_copy(
            src_ref=down_src.at[row],
            dst_ref=down_buf.at[row],
            send_sem=down_send.at[row],
            recv_sem=down_recv.at[row],
            device_id={"tile": device},
            device_id_type=MESH,
        )

    def destination(step):
        is_last = spot // last
        return is_last * step + (1 - is_last) * ((spot + step) % last if step else last)

    def push(step):
        target = destination(step)
        total = day_total(target)

        @pl.when(target == spot)
        def _():
            out_ref[0] = total

        @pl.when(target != spot)
        def _():
            send_buf[target] = total.astype(jnp.bfloat16)
            tile_copy(target, spot).start()

    for turn in range(group):
        target = destination(turn)
        products((target + BELOW) % group, target)
        for step in range(1, days):
            day_copy(step, target).start()
        if turn:
            push(turn - 1)

    @pl.when(is_top)
    def _():
        products(group, group)
        for step in range(1, days):
            day_copy(step, group).start()

    push(last)

    @pl.when(is_top)
    def _():
        total = day_total(group)

        @pl.when(spot < last)
        def _():
            send_buf[group] = total.astype(jnp.bfloat16)
            top_copy(base + last, spot).start()

        @pl.when(spot == last)
        def _():
            part_ref[group, day] = total

    for offset in range(last, 0, -1):
        tile_copy(spot, mixed(spot, offset)).wait_recv()
    sends_down = has_below & (spot == last)
    takes_down = has_above & (spot == last)
    for row in range(rows_dev):
        total = out_ref[0, row]
        for offset in range(last, 0, -1):
            total = total + recv_buf[mixed(spot, offset), row].astype(jnp.float32)
        out_ref[0, row] = total

        @pl.when(sends_down)
        def _():
            down_src[row] = total.astype(jnp.bfloat16)
            down_copy(row, here - group).start()

    @pl.when(takes_down)
    def _():
        for row in range(rows_dev):
            down_copy(row, here).wait_recv()
            out_ref[0, row] = down_buf[row].astype(jnp.float32)

    @pl.when(is_top & (spot == last))
    def _():
        total = part_ref[group, day]
        for slot in range(last):
            top_copy(here, slot).wait_recv()
            total = total + top_buf[slot].astype(jnp.float32)
        out_ref[0] = total

    @pl.when(is_top & (spot < last))
    def _():
        top_copy(base + last, spot).wait_send()

    @pl.when(sends_down)
    def _():
        for row in range(rows_dev):
            down_copy(row, here - group).wait_send()

    for offset in range(last, 0, -1):
        tile_copy(mixed(spot, offset), spot).wait_send()
    for offset in range(last, -1, -1):
        for step in range(1, days):
            day_copy(step, offset).wait_send()

    @pl.when(is_top)
    def _():
        for step in range(1, days):
            day_copy(step, group).wait_send()


def per_device(tiles, days, spectra, band_low, band_high, pair_list):
    own = spectra[0]
    channels, parts, segments, bins = own.shape
    group = segments
    chans = channels // BLK_DEV
    rows_dev = pair_list.shape[0]
    lags = days
    norm_factor = 1.0 / math.sqrt(segments * bins * days)
    slice_shape = (parts, BLK_DEV, chans, bins)
    raw = jnp.transpose(own.reshape(BLK_DEV, chans, parts, segments, bins), (3, 2, 0, 1, 4))

    chunks = 2 * BLK_DEV
    block_shape = (rows_dev, chans, chans)
    gathered_shape = (BELOW + group, 8, 128)
    return pl.pallas_call(
        functools.partial(correlate_kernel, tiles, days, group, norm_factor),
        out_shape=jax.ShapeDtypeStruct((1,) + block_shape, jnp.float32),
        in_specs=[SMEM, SMEM, VMEM, VMEM, pl.BlockSpec(memory_space=pl.ANY)],
        out_specs=VMEM,
        scratch_shapes=[
            pltpu.VMEM((segments,) + slice_shape, jnp.bfloat16),
            pltpu.SemaphoreType.DMA((group, BLK_DEV)),
            pltpu.VMEM((segments,) + slice_shape, jnp.bfloat16),
            pltpu.VMEM((bins, bins), jnp.bfloat16),
            pltpu.VMEM((group + REACH,) + slice_shape, jnp.bfloat16),
            pltpu.VMEM(gathered_shape, jnp.int32),
            pltpu.SMEM(gathered_shape, jnp.int32),
            pltpu.VMEM(((group + REACH) * BLK_DEV, parts, lags * chans, bins), jnp.bfloat16),
            pltpu.VMEM((group + 1, lags) + block_shape, jnp.float32),
            pltpu.VMEM((days - 1, group + 1) + block_shape, jnp.float32),
            pltpu.VMEM((group + 1,) + block_shape, jnp.bfloat16),
            pltpu.VMEM((group,) + block_shape, jnp.bfloat16),
            pltpu.VMEM((group - 1,) + block_shape, jnp.bfloat16),
            pltpu.VMEM(block_shape, jnp.bfloat16),
            pltpu.VMEM(block_shape, jnp.bfloat16),
            pltpu.SemaphoreType.DMA((group - 1, chunks)),
            pltpu.SemaphoreType.DMA((group - 1, chunks)),
            pltpu.SemaphoreType.DMA((REACH, chunks)),
            pltpu.SemaphoreType.DMA((REACH, chunks)),
            pltpu.SemaphoreType.DMA((group - 1,)),
            pltpu.SemaphoreType.DMA((group - 1,)),
            pltpu.SemaphoreType.DMA,
            pltpu.SemaphoreType.DMA,
            pltpu.SemaphoreType.DMA,
            pltpu.SemaphoreType.DMA((days - 1, group + 1)),
            pltpu.SemaphoreType.DMA((days - 1, group + 1)),
            pltpu.SemaphoreType.DMA((group,)),
            pltpu.SemaphoreType.DMA((group,)),
            pltpu.SemaphoreType.DMA,
            pltpu.SemaphoreType.DMA((group - 1,)),
            pltpu.SemaphoreType.DMA((rows_dev,)),
            pltpu.SemaphoreType.DMA((rows_dev,)),
        ],
        compiler_params=pltpu.CompilerParams(
            collective_id=0, has_side_effects=True, vmem_limit_bytes=63 * 1024 * 1024
        ),
    )(band_low, band_high, pair_list.T, jnp.asarray(phase_tables(lags, bins)), raw)


def solution(mesh):
    placed = (P("day", "tile", None, None, None), P("tile"), P("tile"), P("tile", None))
    return jax.shard_map(
        functools.partial(per_device, mesh.shape["tile"], mesh.shape["day"]),
        mesh=mesh,
        in_specs=placed,
        out_specs=P("day", "tile", None, None),
        check_vma=False,
    )
```
